32 devices in a mesh: tm: 16 (over z, y, x), dp: 2 (over core).
Axes of the slice: x: 2, y: 2, z: 4, core: 2. Of those that a mesh axis runs over, the one named last changes fastest.
Arguments:
- state_feats: bfloat16 [128, 64, 256], P('dp', 'tm'), may hold values from -6 to 6
- achieved: bfloat16 [128, 64, 512], P('dp', 'tm'), may hold values from -6 to 6
- offsets: int32 [128, 64], P('dp', 'tm'), may hold values from 0 to 63, as said below
- w_in: bfloat16 [768, 2048], replicated, may hold values from -0.21875 to 0.21875
- b_in: float32 [2048], replicated, may hold values from -3 to 3
- w_out: float32 [2048], replicated, may hold values from -0.75 to 0.75
- b_out: float32 [1], replicated, may hold values from -1 to 1
Outputs:
- td_error: float32 [128, 64], P('dp', 'tm')
- grad_w_in: float32 [768, 2048], P(('tm', 'dp'))
- grad_b_in: float32 [2048], replicated
- grad_w_out: float32 [2048], replicated
- grad_b_out: float32 [1], replicated
The draws below stay inside these ranges and needn't reach their ends.
Inputs may be any that keep to these rules, and one draw needn't show every extreme that they name: t + offsets[e, t] <= 63. The transitions held by one device (one index of dp and of tm) ask at most 4 of their goals from any other single index of tm; every device whose tm index is below the last asks exactly 4 goals from the last index, all of them at time 64 - 1.
All inputs are finite; a program needn't handle non-finite values.
Results may differ from the reference program's by a relative error of at most 0.0024.
The reference program's roundings to bfloat16 on the way (of `goal`, `inputs`, `hidden` and `grad_low`) count: a program that leaves them out, or rounds other values in their place, can miss the bound.
Values may be sent and summed in bfloat16 or wider, within the bound.
A program may use at most 64 MiB of HBM per device.

```python
import math
import jax
import jax.numpy as jnp
from jax import lax

S = 256
G = 512
H = 2048
STEPS = 4
EP_DEV = 64
CAP = 4
EP_LEN = 64
EPISODES = 128


def draw_offsets(key, part):
    tm_count = EP_LEN // STEPS
    dp_count = EPISODES // EP_DEV
    rows = EP_DEV * STEPS
    key_far, key_near, key_final = jax.random.split(key, 3)
    shape = (EPISODES, EP_LEN)
    times = jnp.broadcast_to(jnp.arange(EP_LEN, dtype=jnp.int32)[None, :], shape)
    future = times + jax.random.randint(key_far, shape, 0, EP_LEN - times)
    home = times // STEPS
    nearby = times + jax.random.randint(key_near, shape, 0, (home + 1) * STEPS - times)

    def blocks(values):
        return values.reshape(dp_count, EP_DEV, tm_count, STEPS).transpose(0, 2, 1, 3).reshape(dp_count, tm_count, rows)

    def unblock(values):
        return values.reshape(dp_count, tm_count, EP_DEV, STEPS).transpose(0, 2, 1, 3).reshape(EPISODES, EP_LEN)
    owner_rows = blocks(future // STEPS)
    home_rows = blocks(home)
    remote = (owner_rows != home_rows) & (owner_rows != tm_count - 1)
    peers = jnp.arange(tm_count, dtype=jnp.int32)
    hits = ((owner_rows[..., None] == peers) & remote[..., None]).astype(jnp.int32)
    rank = jnp.sum((jnp.cumsum(hits, axis=2) - 1) * hits, axis=3)
    keep = remote & (rank < CAP)
    scores = jax.random.randint(key_final, (dp_count, tm_count, rows), 0, 1 << 20) * rows + jnp.arange(rows, dtype=jnp.int32)
    order = jnp.argsort(jnp.argsort(scores, axis=2), axis=2)
    final = (order < CAP) & (home_rows < tm_count - 1)
    chosen = jnp.where(final, EP_LEN - 1, jnp.where(keep, blocks(future), blocks(nearby)))
    return (unblock(chosen) - times).astype(jnp.int32)


def with_spikes(array, key, source, target, blocks, factor):
    def block_of(axis_at):
        return (jnp.arange(array.shape[axis_at]) // (array.shape[axis_at] // blocks)).reshape((-1,) + (1,) * (array.ndim - 1 - axis_at))

    one_side = jax.random.permutation(key, blocks)[block_of(target)]
    second = (block_of(target) + blocks // 2) % blocks
    return jnp.where((block_of(source) == one_side) | (block_of(source) == second), factor * array, array)


def shard_levels(stream_key, shape, cuts, least, high):
    def one(position, blocks):
        heights = jax.random.uniform(jax.random.fold_in(jax.random.fold_in(stream_key, 6), position), (blocks,), jnp.float32, least / len(cuts), high / len(cuts))
        return jnp.repeat(jnp.exp(heights), shape[position] // blocks).reshape((-1,) + (1,) * (len(shape) - position - 1))

    loudness = one(*cuts[0])
    for cut in cuts[1:]:
        loudness = loudness * one(*cut)
    return loudness


def normal_values(stream_key, dims, spread, bound, shards=(), kind=jnp.bfloat16):
    result = jax.random.normal(stream_key, dims, jnp.float32) * spread
    if len(shards) > 0:
        result = shard_levels(stream_key, dims, shards, -0.22, 0.18) * result
    return jnp.clip(result, min=-bound, max=bound).astype(kind)


def bell_draw_with(stream_key, extent, deviation, reach, shards, heavy, kind=jnp.bfloat16):
    drawn = deviation * jax.random.normal(stream_key, extent, jnp.float32)
    if shards:
        drawn = drawn * shard_levels(stream_key, extent, shards, -0.22, 0.18)
    return jnp.clip(with_spikes(drawn, jax.random.fold_in(stream_key, 3), *heavy), -reach, reach).astype(kind)


def setup_inputs(seed: int = 0) -> dict:
    streams_of = jax.random.split(jax.random.key(seed), 8)
    return {
        "state_feats": bell_draw_with(streams_of[0], (EPISODES, EP_LEN, S), 1.0, 6.0, ((0, 2), (1, 16)), (1, 2, 16, 2.0)),
        "achieved": bell_draw_with(streams_of[1], (EPISODES, EP_LEN, G), 1.0, 6.0, ((0, 2), (1, 16)), (1, 2, 16, 2.0)),
        "offsets": draw_offsets(jax.random.fold_in(streams_of[7], 71), 0),
        "w_in": normal_values(streams_of[3], (S + G, H), (S + G) ** -0.5, 0.21875),
        "b_in": normal_values(streams_of[4], (H,), 0.5, 3.0, (), jnp.float32),
        "w_out": normal_values(streams_of[5], (H,), 64 ** -0.5, 0.75, (), jnp.float32),
        "b_out": jnp.clip(jax.random.uniform(streams_of[6], (1,), jnp.float32, -1.0, 1.0), -1.0, 1.0),
    }


def reference(state_feats, achieved, offsets, w_in, b_in, w_out, b_out):
    times = jnp.arange(EP_LEN, dtype=jnp.int32)
    target = (times[None, :] + offsets).astype(jnp.int32)
    goal = jnp.take_along_axis(achieved, target[:, :, None], axis=1)
    scale = 1.0 / math.sqrt(EPISODES * EP_LEN)

    def episode_step(carry, parts):
        feats, reached, wanted = parts
        inputs = jnp.concatenate([feats, wanted], axis=1)
        pre = jnp.dot(inputs, w_in, preferred_element_type=jnp.float32) + b_in
        hidden = jax.nn.silu(pre).astype(jnp.bfloat16)
        hidden_wide = hidden.astype(jnp.float32)
        value = jnp.dot(hidden_wide, w_out, precision=lax.Precision.HIGHEST) + b_out[0]
        diff = reached.astype(jnp.float32) - wanted.astype(jnp.float32)
        reward = -lax.optimization_barrier(jnp.mean(diff * diff, axis=1))
        error = value - reward
        grad_value = error * scale
        sig = jax.nn.sigmoid(pre)
        grad_pre = grad_value[:, None] * w_out[None, :] * (sig * (1.0 + pre * (1.0 - sig)))
        grad_low = grad_pre.astype(jnp.bfloat16)
        gw_in = lax.dot_general(inputs, grad_low, (((0,), (0,)), ((), ())), preferred_element_type=jnp.float32)
        gb_in = lax.optimization_barrier(jnp.sum(grad_pre, axis=0))
        gw_out = jnp.dot(grad_value, hidden_wide, precision=lax.Precision.HIGHEST)
        gb_out = lax.optimization_barrier(jnp.sum(grad_value, keepdims=True))
        return ((carry[0] + gw_in, carry[1] + gb_in, carry[2] + gw_out, carry[3] + gb_out), error)
    start = (jnp.zeros((S + G, H), jnp.float32), jnp.zeros((H,), jnp.float32), jnp.zeros((H,), jnp.float32), jnp.zeros((1,), jnp.float32))
    totals, errors = lax.scan(episode_step, start, (state_feats, achieved, goal))
    return (errors, totals[0], totals[1], totals[2], totals[3])
```

```python
import functools
import math

import jax
import jax.numpy as jnp
from jax import lax
from jax.experimental import pallas as pl
from jax.experimental.pallas import tpu as pltpu
from jax.sharding import PartitionSpec as P

CAP = 4
LANES = 128
GROUP = 8
MESH = pl.DeviceIdType.MESH
BF16 = jnp.bfloat16
F32 = jnp.float32


def iota(shape, axis):
    return lax.broadcasted_iota(jnp.int32, shape, axis)


def dot(a, b):
    return jnp.dot(a, b, preferred_element_type=F32)


def dot_rows(a, b):
    return lax.dot_general(a, b, (((0,), (0,)), ((), ())), preferred_element_type=F32)


def onehot(mask):
    return jnp.where(mask, 1.0, 0.0).astype(BF16)


def wait_bytes(ref, sem):
    pltpu.make_async_copy(ref, ref, sem).wait()


def kernel(dims, sf_ref, ach_ref, off_ref, w_hbm, b_ref, wo_ref, bo_ref,
           err_ref, gw_ref, gb_ref, gwo_ref, gbo_ref,
           w, pre, hid, low, low_send, xt, req_send, req_recv, resp_send, resp_recv,
           big_send, big_recv, own, sm_send, sm_recv, all_send, all_recv,
           w_sem, pair_send, pair_recv, s_sem, r_sem):
    tm_n, dp_n, steps, rdev, rpad = dims
    n = tm_n * dp_n
    rows, feat = sf_ref.shape
    goal_w = ach_ref.shape[1]
    hidden_n = wo_ref.shape[1]
    half = hidden_n // dp_n
    inner = feat + goal_w
    nc = goal_w // LANES
    slots = CAP * nc
    peers = tm_n - 1
    tm = lax.axis_index("tm")
    dp = lax.axis_index("dp")
    me = tm * dp_n + dp
    partner = (tm, 1 - dp)

    w_copy = pltpu.make_async_copy(w_hbm, w, w_sem)
    w_copy.start()

    barrier = pltpu.get_barrier_semaphore()

    def greet(k, c):
        dev = lax.rem(me + k, n)
        pl.semaphore_signal(barrier, inc=1, device_id=(dev // dp_n, lax.rem(dev, dp_n)), device_id_type=MESH)
        return c

    lax.fori_loop(1, n, greet, 0)

    def remote(src, dst, ss, rs, dev):
        return pltpu.make_async_remote_copy(
            src_ref=src, dst_ref=dst, send_sem=ss, recv_sem=rs, device_id=dev, device_id_type=MESH)

    r = iota((1, rows), 1)
    ahead = lax.rem(r, steps) + off_ref[...]
    rel = ahead // steps
    pos = (r // steps) * steps + lax.rem(ahead, steps)
    i = iota((peers * slots, rows), 0)
    hits = (i // slots + 1) == rel
    tri = onehot(iota((rows, rows), 0) <= iota((rows, rows), 1))
    rank = dot(onehot(hits), tri).astype(jnp.int32)
    sel = hits & (rank == lax.rem(i, CAP) + 1)
    want = jnp.sum(jnp.where(sel, pos + 1, 0).astype(F32), axis=1, keepdims=True) - 1.0
    req_send[...] = jnp.broadcast_to(want, (peers * slots, LANES)).astype(BF16).reshape(peers, slots, LANES)

    pl.semaphore_wait(barrier, n - 1)

    def ask(k, c):
        remote(req_send.at[k - 1], req_recv.at[k - 1], s_sem.at[0], r_sem.at[0],
               (lax.rem(tm + k, tm_n), dp)).start()
        return c

    lax.fori_loop(1, tm_n, ask, 0)

    table = ach_ref[...]
    near = onehot((iota((rows, rows), 0) == pos) & (rel == 0))
    goal_near = dot_rows(near, table)
    sf = sf_ref[...]
    if rpad == rdev:
        xt[0, 0:feat, :] = sf.T
    w_copy.wait()
    cw = 256
    chunks = hidden_n // cw

    def first(j, c):
        cols = pl.ds(pl.multiple_of(j * cw, cw), cw)
        pre[:, cols] = dot(sf, w[0:feat, cols]) + b_ref[:, cols]
        return c

    wait_bytes(req_recv, r_sem.at[0])
    asked = req_recv[...].reshape(peers * slots, LANES).astype(F32)
    asked = jnp.concatenate([asked] * (rows // LANES), axis=1).astype(jnp.int32)
    found = asked == iota((peers * slots, rows), 1)
    part = lax.rem(i, slots) // CAP
    picked = jnp.zeros((peers * slots, LANES), F32)
    for c in range(nc):
        picked = picked + dot(onehot(found & (part == c)), table[:, c * LANES:(c + 1) * LANES])
    resp_send[...] = picked.astype(BF16).reshape(peers, slots, LANES)

    def answer(k, c):
        remote(resp_send.at[k - 1], resp_recv.at[k - 1], s_sem.at[1], r_sem.at[1],
               (lax.rem(tm - k + tm_n, tm_n), dp)).start()
        return c

    lax.fori_loop(1, tm_n, answer, 0)
    lax.fori_loop(0, chunks, first, 0)
    wait_bytes(resp_recv, r_sem.at[1])
    fetched = resp_recv[...].reshape(peers * slots, LANES)
    far = [dot_rows(onehot(sel & (part == c)), fetched) for c in range(nc)]
    goal_wide = goal_near + jnp.concatenate(far, axis=1)
    goal = goal_wide.astype(BF16)

    if rpad == rdev:
        xt[0, feat:inner, :] = goal.T
    else:
        x = jnp.concatenate([sf, goal], axis=1)
        o = iota((n * rpad, inner), 0)
        place = (o // rpad) * rdev + lax.rem(o, rpad)
        place = jnp.where(lax.rem(o, rpad) < rdev, place, -1)
        xt[0] = lax.dot_general(onehot(place == iota((n * rpad, inner), 1)), x,
                                (((1,), (1,)), ((), ())), preferred_element_type=F32).astype(BF16)
    x_copy = remote(xt.at[0], xt.at[1], pair_send.at[0], pair_recv.at[0], partner)
    x_copy.start()

    diff = table.astype(F32) - goal_wide
    reward = -jnp.mean(diff * diff, axis=1, keepdims=True)

    def second(j, acc):
        cols = pl.ds(pl.multiple_of(j * cw, cw), cw)
        p = pre[:, cols] + dot(goal, w[feat:inner, cols])
        s = 1.0 / (1.0 + jnp.exp(-p))
        wo = wo_ref[:, cols]
        h = (p * s).astype(BF16)
        hid[:, cols] = h
        pre[:, cols] = wo * (s * (1.0 + p * (1.0 - s)))
        v = h.astype(F32) * wo
        for q in range(cw // LANES):
            acc = acc + v[:, q * LANES:(q + 1) * LANES]
        return acc

    acc = lax.fori_loop(0, chunks, second, jnp.zeros((rows, LANES), F32))
    value = jnp.sum(acc, axis=1, keepdims=True) + bo_ref[...]
    error = value - reward
    diag = iota((rows, rows), 0) == iota((rows, rows), 1)
    err_ref[...] = jnp.sum(jnp.where(diag, error, 0.0), axis=0, keepdims=True)
    gv = error * (1.0 / math.sqrt(rows * n))
    gbo = jnp.broadcast_to(jnp.sum(gv, axis=0, keepdims=True), (1, LANES))

    per = cw // LANES
    hv = hidden_n // LANES

    def back(which, out):
        def step(j, c):
            col = pl.multiple_of(which * half + j * cw, cw)
            cols = pl.ds(col, cw)
            g = gv * pre[:, cols]
            out[:, pl.ds(pl.multiple_of(j * cw, cw), cw)] = g.astype(BF16)
            gs = jnp.sum(g, axis=0, keepdims=True)
            hs = jnp.sum(gv * hid[:, cols].astype(F32), axis=0, keepdims=True)
            at = which * (half // LANES) + j * per
            for q in range(per):
                lanes = slice(q * LANES, (q + 1) * LANES)
                sm_send[at + q] = jnp.concatenate([gs[:, lanes], gbo], axis=1)
                sm_send[hv + at + q] = jnp.concatenate([hs[:, lanes], gbo], axis=1)
            return c
        return step

    lax.fori_loop(0, half // cw, back(1 - dp, low_send), 0)
    l_copy = remote(low_send, low.at[1], pair_send.at[1], pair_recv.at[1], partner)
    l_copy.start()
    lax.fori_loop(0, half // cw, back(dp, low.at[0]), 0)

    owners = 2 * hv

    def small(k, c):
        dev = lax.rem(me + k, n)

        def go():
            remote(sm_send.at[dev], sm_recv.at[k - 1], s_sem.at[2], r_sem.at[2],
                   (dev // dp_n, lax.rem(dev, dp_n))).start()
        if owners == n:
            go()
        else:
            pl.when(dev < owners)(go)
        return c

    lax.fori_loop(1, n, small, 0)
    x_copy.wait_recv()
    l_copy.wait_recv()

    block = GROUP * rpad
    groups = n // GROUP

    def form(g, c):
        base = lax.rem(me // GROUP + 1 + g, groups)
        at = pl.ds(pl.multiple_of(base * block, block), block)
        p = dot(xt[0, at, :], low[0]) + dot(xt[1, at, :], low[1])
        for d in range(GROUP):
            dev = base * GROUP + d
            blk = p[d * rpad:(d + 1) * rpad]
            blk = jnp.concatenate([blk[:, :half // 2], blk[:, half // 2:]], axis=0)
            big_send[dev] = blk.astype(BF16)

            @pl.when(dev == me)
            def _():
                own[...] = blk

            @pl.when(dev != me)
            def _():
                k = lax.rem(dev - me + n, n)
                remote(big_send.at[dev], big_recv.at[k - 1], s_sem.at[3], r_sem.at[3],
                       (dev // dp_n, lax.rem(dev, dp_n))).start()
        return c

    lax.fori_loop(0, groups, form, 0)

    def total():
        wait_bytes(sm_recv, r_sem.at[2])
        all_send[...] = sm_send[me] + jnp.sum(sm_recv[...], axis=0)
        all_recv[me] = all_send[...]

        def tell(k, c):
            dev = lax.rem(me + k, n)
            remote(all_send, all_recv.at[me], s_sem.at[4], r_sem.at[4],
                   (dev // dp_n, lax.rem(dev, dp_n))).start()
            return c

        lax.fori_loop(1, n, tell, 0)

    if owners == n:
        total()
        wait_bytes(all_recv.at[pl.ds(0, n - 1)], r_sem.at[4])
    else:
        pl.when(me < owners)(total)

        @pl.when(me < owners)
        def _():
            wait_bytes(all_recv.at[pl.ds(0, owners - 1)], r_sem.at[4])

        @pl.when(me >= owners)
        def _():
            wait_bytes(all_recv.at[pl.ds(0, owners)], r_sem.at[4])
    for q in range(hv):
        lanes = slice(q * LANES, (q + 1) * LANES)
        gb_ref[:, lanes] = all_recv[q][:, :LANES]
        gwo_ref[:, lanes] = all_recv[hv + q][:, :LANES]
    gbo_ref[...] = all_recv[0][:, LANES:LANES + 1]

    wait_bytes(big_recv, r_sem.at[3])

    def add(k, c):
        same, other = c
        return same + big_recv[2 * k + 1].astype(F32), other + big_recv[2 * k].astype(F32)

    q4 = half // 4
    for q in range(2):
        lanes = slice(q * q4, (q + 1) * q4)

        def add(k, c):
            same, other = c
            return (same + big_recv[2 * k + 1, :, lanes].astype(F32),
                    other + big_recv[2 * k, :, lanes].astype(F32))

        same, other = lax.fori_loop(
            0, tm_n - 1, add, (own[:, lanes], jnp.zeros((2 * rpad, q4), F32)))
        other = other + big_recv[n - 2, :, lanes].astype(F32)
        for which, val in ((dp, same), (1 - dp, other)):
            for z in range(2):
                col = pl.multiple_of(which * half + z * (half // 2) + q * q4, LANES)
                gw_ref[:, pl.ds(col, q4)] = val[z * rpad:z * rpad + rdev]

    wait_bytes(req_send, s_sem.at[0])
    wait_bytes(resp_send, s_sem.at[1])
    x_copy.wait_send()
    l_copy.wait_send()
    if owners == n:
        wait_bytes(sm_send.at[pl.ds(0, n - 1)], s_sem.at[2])
        wait_bytes(all_recv.at[pl.ds(0, n - 1)], s_sem.at[4])
    else:
        @pl.when(me < owners)
        def _():
            wait_bytes(sm_send.at[pl.ds(0, owners - 1)], s_sem.at[2])
            wait_bytes(sm_recv, s_sem.at[4])

        @pl.when(me >= owners)
        def _():
            wait_bytes(sm_send.at[pl.ds(0, owners)], s_sem.at[2])
    wait_bytes(big_send.at[pl.ds(0, n - 1)], s_sem.at[3])


def body(tm_n, dp_n, state_feats, achieved, offsets, w_in, b_in, w_out, b_out):
    ep_dev, steps, goal_w = achieved.shape
    feat = state_feats.shape[2]
    rows = ep_dev * steps
    inner, hidden_n = w_in.shape
    n = tm_n * dp_n
    half = hidden_n // dp_n
    rdev = inner // n
    rpad = -(-rdev // 8) * 8
    slots = CAP * (goal_w // LANES)
    owners = 2 * hidden_n // LANES
    assert dp_n == 2 and rows <= 256 and owners <= n and n % GROUP == 0
    vmem = pl.BlockSpec(memory_space=pltpu.VMEM)
    out = pl.pallas_call(
        functools.partial(kernel, (tm_n, dp_n, steps, rdev, rpad)),
        out_shape=(
            jax.ShapeDtypeStruct((1, rows), F32),
            jax.ShapeDtypeStruct((rdev, hidden_n), F32),
            jax.ShapeDtypeStruct((1, hidden_n), F32),
            jax.ShapeDtypeStruct((1, hidden_n), F32),
            jax.ShapeDtypeStruct((1, 1), F32),
        ),
        in_specs=[vmem] * 3 + [pl.BlockSpec(memory_space=pl.ANY)] + [vmem] * 3,
        out_specs=[vmem] * 5,
        scratch_shapes=[
            pltpu.VMEM((inner, hidden_n), BF16),
            pltpu.VMEM((rows, hidden_n), F32),
            pltpu.VMEM((rows, hidden_n), BF16),
            pltpu.VMEM((2, rows, half), BF16),
            pltpu.VMEM((rows, half), BF16),
            pltpu.VMEM((2, n * rpad, rows), BF16),
            pltpu.VMEM((tm_n - 1, slots, LANES), BF16),
            pltpu.VMEM((tm_n - 1, slots, LANES), BF16),
            pltpu.VMEM((tm_n - 1, slots, LANES), BF16),
            pltpu.VMEM((tm_n - 1, slots, LANES), BF16),
            pltpu.VMEM((n, 2 * rpad, half // 2), BF16),
            pltpu.VMEM((n - 1, 2 * rpad, half // 2), BF16),
            pltpu.VMEM((2 * rpad, half // 2), F32),
            pltpu.VMEM((owners, 1, 2 * LANES), F32),
            pltpu.VMEM((n - 1, 1, 2 * LANES), F32),
            pltpu.VMEM((1, 2 * LANES), F32),
            pltpu.VMEM((owners, 1, 2 * LANES), F32),
            pltpu.SemaphoreType.DMA,
            pltpu.SemaphoreType.DMA((2,)),
            pltpu.SemaphoreType.DMA((2,)),
            pltpu.SemaphoreType.DMA((5,)),
            pltpu.SemaphoreType.DMA((5,)),
        ],
        compiler_params=pltpu.CompilerParams(
            collective_id=0, has_side_effects=True, vmem_limit_bytes=60 * 1024 * 1024),
    )(state_feats.reshape(rows, feat), achieved.reshape(rows, goal_w), offsets.reshape(1, rows),
      w_in, b_in.reshape(1, hidden_n), w_out.reshape(1, hidden_n), b_out.reshape(1, 1))
    err, gw, gb, gwo, gbo = out
    return (err.reshape(ep_dev, steps), gw, gb.reshape(hidden_n), gwo.reshape(hidden_n), gbo.reshape(1))


def solution(mesh):
    in_specs = (P("dp", "tm", None), P("dp", "tm", None), P("dp", "tm"), P(), P(), P(), P())
    out_specs = (P("dp", "tm"), P(("tm", "dp"), None), P(), P(), P())
    step = functools.partial(body, mesh.shape["tm"], mesh.shape["dp"])
    return jax.shard_map(step, mesh=mesh, in_specs=in_specs, out_specs=out_specs, check_vma=False)
```

```python
import functools
import math

import jax
import jax.numpy as jnp
from jax import lax
from jax.experimental import pallas as pl
from jax.experimental.pallas import tpu as pltpu
from jax.sharding import PartitionSpec as P

CAP = 4
LANES = 128
GROUP = 8
MESH = pl.DeviceIdType.MESH
BF16 = jnp.bfloat16
F32 = jnp.float32


def iota(shape, axis):
    return lax.broadcasted_iota(jnp.int32, shape, axis)


def dot(a, b):
    return jnp.dot(a, b, preferred_element_type=F32)


def dot_rows(a, b):
    return lax.dot_general(a, b, (((0,), (0,)), ((), ())), preferred_element_type=F32)


def onehot(mask):
    return jnp.where(mask, 1.0, 0.0).astype(BF16)


def wait_bytes(ref, sem):
    pltpu.make_async_copy(ref, ref, sem).wait()


def kernel(dims, sf_hbm, ach_hbm, off_hbm, w_hbm, b_hbm, wo_hbm, bo_ref,
           err_ref, gw_ref, gb_ref, gwo_ref, gbo_ref,
           sf_ref, ach_ref, off_ref, b_ref, wo_ref, w, pre, hid, low, low_send, xt, req_send, req_recv, resp_send, resp_recv,
           big_send, big_recv, own, sm_send, sm_recv, all_send, all_recv,
           in_sem, pair_send, pair_recv, s_sem, r_sem):
    tm_n, dp_n, steps, rdev, rpad = dims
    n = tm_n * dp_n
    ep_dev, _, feat = sf_ref.shape
    rows = ep_dev * steps
    goal_w = ach_ref.shape[2]
    hidden_n = wo_ref.shape[1]
    half = hidden_n // dp_n
    inner = feat + goal_w
    nc = goal_w // LANES
    slots = CAP * nc
    peers = tm_n - 1
    tm = lax.axis_index("tm")
    dp = lax.axis_index("dp")
    me = tm * dp_n + dp
    partner = (tm, 1 - dp)

    loads = [pltpu.make_async_copy(src, dst, in_sem.at[j]) for j, (src, dst) in enumerate((
        (off_hbm, off_ref), (ach_hbm, ach_ref), (sf_hbm, sf_ref), (b_hbm, b_ref), (wo_hbm, wo_ref),
        (w_hbm, w)))]
    for load in loads:
        load.start()

    barrier = pltpu.get_barrier_semaphore()

    def greet(k, c):
        dev = lax.rem(me + k, n)
        pl.semaphore_signal(barrier, inc=1, device_id=(dev // dp_n, lax.rem(dev, dp_n)), device_id_type=MESH)
        return c

    lax.fori_loop(1, n, greet, 0)

    def remote(src, dst, ss, rs, dev):
        return pltpu.make_async_remote_copy(
            src_ref=src, dst_ref=dst, send_sem=ss, recv_sem=rs, device_id=dev, device_id_type=MESH)

    loads[0].wait()

    r = iota((1, rows), 1)
    spread = onehot(iota((ep_dev, rows), 0) == iota((ep_dev, rows), 1) // steps)
    off = off_ref[...]
    off = (dot((off // LANES).astype(F32).astype(BF16), spread) * LANES
           + dot(lax.rem(off, LANES).astype(F32).astype(BF16), spread)).astype(jnp.int32)
    off = jnp.sum(jnp.where(iota((steps, rows), 0) == lax.rem(r, steps), off, 0), axis=0, keepdims=True)
    ahead = lax.rem(r, steps) + off
    rel = ahead // steps
    pos = (r // steps) * steps + lax.rem(ahead, steps)
    i = iota((peers * slots, rows), 0)
    hits = (i // slots + 1) == rel
    tri = onehot(iota((rows, rows), 0) <= iota((rows, rows), 1))
    rank = dot(onehot(hits), tri).astype(jnp.int32)
    sel = hits & (rank == lax.rem(i, CAP) + 1)
    want = jnp.sum(jnp.where(sel, pos + 1, 0).astype(F32), axis=1, keepdims=True) - 1.0
    req_send[...] = jnp.broadcast_to(want, (peers * slots, LANES)).astype(BF16).reshape(peers, slots, LANES)

    pl.semaphore_wait(barrier, n - 1)

    def ask(k, c):
        remote(req_send.at[k - 1], req_recv.at[k - 1], s_sem.at[0], r_sem.at[0],
               (lax.rem(tm + k, tm_n), dp)).start()
        return c

    lax.fori_loop(1, tm_n, ask, 0)

    loads[1].wait()
    table = ach_ref[...].reshape(rows, goal_w)
    near = onehot((iota((rows, rows), 0) == pos) & (rel == 0))
    goal_near = dot_rows(near, table)
    loads[2].wait()
    sf = sf_ref[...].reshape(rows, feat)
    if rpad == rdev:
        xt[0, 0:feat, :] = sf.T
    for load in loads[3:]:
        load.wait()
    cw = 256
    chunks = hidden_n // cw

    def first(j, c):
        cols = pl.ds(pl.multiple_of(j * cw, cw), cw)
        pre[:, cols] = dot(sf, w[0:feat, cols]) + b_ref[:, cols]
        return c

    wait_bytes(req_recv, r_sem.at[0])
    asked = req_recv[...].reshape(peers * slots, LANES).astype(F32)
    asked = jnp.concatenate([asked] * (rows // LANES), axis=1).astype(jnp.int32)
    found = asked == iota((peers * slots, rows), 1)
    part = lax.rem(i, slots) // CAP
    picked = jnp.zeros((peers * slots, LANES), F32)
    for c in range(nc):
        picked = picked + dot(onehot(found & (part == c)), table[:, c * LANES:(c + 1) * LANES])
    resp_send[...] = picked.astype(BF16).reshape(peers, slots, LANES)

    def answer(k, c):
        remote(resp_send.at[k - 1], resp_recv.at[k - 1], s_sem.at[1], r_sem.at[1],
               (lax.rem(tm - k + tm_n, tm_n), dp)).start()
        return c

    lax.fori_loop(1, tm_n, answer, 0)
    lax.fori_loop(0, chunks, first, 0)
    wait_bytes(resp_recv, r_sem.at[1])
    fetched = resp_recv[...].reshape(peers * slots, LANES)
    far = [dot_rows(onehot(sel & (part == c)), fetched) for c in range(nc)]
    goal_wide = goal_near + jnp.concatenate(far, axis=1)
    goal = goal_wide.astype(BF16)

    if rpad == rdev:
        xt[0, feat:inner, :] = goal.T
    else:
        x = jnp.concatenate([sf, goal], axis=1)
        o = iota((n * rpad, inner), 0)
        place = (o // rpad) * rdev + lax.rem(o, rpad)
        place = jnp.where(lax.rem(o, rpad) < rdev, place, -1)
        xt[0] = lax.dot_general(onehot(place == iota((n * rpad, inner), 1)), x,
                                (((1,), (1,)), ((), ())), preferred_element_type=F32).astype(BF16)
    x_copy = remote(xt.at[0], xt.at[1], pair_send.at[0], pair_recv.at[0], partner)
    x_copy.start()

    diff = table.astype(F32) - goal_wide
    reward = -jnp.mean(diff * diff, axis=1, keepdims=True)

    def second(j, acc):
        cols = pl.ds(pl.multiple_of(j * cw, cw), cw)
        p = pre[:, cols] + dot(goal, w[feat:inner, cols])
        s = 1.0 / (1.0 + jnp.exp(-p))
        wo = wo_ref[:, cols]
        h = (p * s).astype(BF16)
        hid[:, cols] = h
        pre[:, cols] = wo * (s * (1.0 + p * (1.0 - s)))
        v = h.astype(F32) * wo
        for q in range(cw // LANES):
            acc = acc + v[:, q * LANES:(q + 1) * LANES]
        return acc

    acc = lax.fori_loop(0, chunks, second, jnp.zeros((rows, LANES), F32))
    value = jnp.sum(acc, axis=1, keepdims=True) + bo_ref[0]
    error = value - reward
    er = iota((rows, ep_dev), 0)
    home = er // steps == iota((rows, ep_dev), 1)
    for t in range(steps):
        err_ref[t:t + 1, :] = jnp.sum(
            jnp.where(home & (lax.rem(er, steps) == t), error, 0.0), axis=0, keepdims=True)
    gv = error * (1.0 / math.sqrt(rows * n))
    gbo = jnp.broadcast_to(jnp.sum(gv, axis=0, keepdims=True), (1, LANES))

    per = cw // LANES
    hv = hidden_n // LANES

    def back(which, out):
        def step(j, c):
            col = pl.multiple_of(which * half + j * cw, cw)
            cols = pl.ds(col, cw)
            g = gv * pre[:, cols]
            out[:, pl.ds(pl.multiple_of(j * cw, cw), cw)] = g.astype(BF16)
            gs = jnp.sum(g, axis=0, keepdims=True)
            hs = jnp.sum(gv * hid[:, cols].astype(F32), axis=0, keepdims=True)
            at = which * (half // LANES) + j * per
            for q in range(per):
                lanes = slice(q * LANES, (q + 1) * LANES)
                sm_send[at + q] = jnp.concatenate([gs[:, lanes], gbo], axis=1)
                sm_send[hv + at + q] = jnp.concatenate([hs[:, lanes], gbo], axis=1)
            return c
        return step

    lax.fori_loop(0, half // cw, back(1 - dp, low_send), 0)
    l_copy = remote(low_send, low.at[1], pair_send.at[1], pair_recv.at[1], partner)
    l_copy.start()
    lax.fori_loop(0, half // cw, back(dp, low.at[0]), 0)

    owners = 2 * hv

    def small(k, c):
        dev = lax.rem(me + k, n)

        def go():
            remote(sm_send.at[dev], sm_recv.at[k - 1], s_sem.at[2], r_sem.at[2],
                   (dev // dp_n, lax.rem(dev, dp_n))).start()
        if owners == n:
            go()
        else:
            pl.when(dev < owners)(go)
        return c

    lax.fori_loop(1, n, small, 0)
    x_copy.wait_recv()
    l_copy.wait_recv()

    block = GROUP * rpad
    groups = n // GROUP

    def form(g, c):
        base = lax.rem(me // GROUP + 1 + g, groups)
        at = pl.ds(pl.multiple_of(base * block, block), block)
        p = dot(xt[0, at, :], low[0]) + dot(xt[1, at, :], low[1])
        for d in range(GROUP):
            dev = base * GROUP + d
            blk = p[d * rpad:(d + 1) * rpad]
            blk = jnp.concatenate([blk[:, :half // 2], blk[:, half // 2:]], axis=0)
            big_send[dev] = blk.astype(BF16)

            @pl.when(dev == me)
            def _():
                own[...] = blk

            @pl.when(dev != me)
            def _():
                k = lax.rem(dev - me + n, n)
                remote(big_send.at[dev], big_recv.at[k - 1], s_sem.at[3], r_sem.at[3],
                       (dev // dp_n, lax.rem(dev, dp_n))).start()
        return c

    lax.fori_loop(0, groups, form, 0)

    def total():
        wait_bytes(sm_recv, r_sem.at[2])
        all_send[...] = sm_send[me] + jnp.sum(sm_recv[...], axis=0)
        all_recv[me] = all_send[...]

        def tell(k, c):
            dev = lax.rem(me + k, n)
            remote(all_send, all_recv.at[me], s_sem.at[4], r_sem.at[4],
                   (dev // dp_n, lax.rem(dev, dp_n))).start()
            return c

        lax.fori_loop(1, n, tell, 0)

    if owners == n:
        total()
        wait_bytes(all_recv.at[pl.ds(0, n - 1)], r_sem.at[4])
    else:
        pl.when(me < owners)(total)

        @pl.when(me < owners)
        def _():
            wait_bytes(all_recv.at[pl.ds(0, owners - 1)], r_sem.at[4])

        @pl.when(me >= owners)
        def _():
            wait_bytes(all_recv.at[pl.ds(0, owners)], r_sem.at[4])
    for q in range(hv):
        lanes = slice(q * LANES, (q + 1) * LANES)
        gb_ref[:, lanes] = all_recv[q][:, :LANES]
        gwo_ref[:, lanes] = all_recv[hv + q][:, :LANES]
    gbo_ref[...] = all_recv[0][:, LANES:LANES + 1]

    wait_bytes(big_recv, r_sem.at[3])

    def add(k, c):
        same, other = c
        return same + big_recv[2 * k + 1].astype(F32), other + big_recv[2 * k].astype(F32)

    q4 = half // 4
    for q in range(2):
        lanes = slice(q * q4, (q + 1) * q4)

        def add(k, c):
            same, other = c
            return (same + big_recv[2 * k + 1, :, lanes].astype(F32),
                    other + big_recv[2 * k, :, lanes].astype(F32))

        same, other = lax.fori_loop(
            0, tm_n - 1, add, (own[:, lanes], jnp.zeros((2 * rpad, q4), F32)))
        other = other + big_recv[n - 2, :, lanes].astype(F32)
        for which, val in ((dp, same), (1 - dp, other)):
            for z in range(2):
                col = pl.multiple_of(which * half + z * (half // 2) + q * q4, LANES)
                gw_ref[:, pl.ds(col, q4)] = val[z * rpad:z * rpad + rdev]

    wait_bytes(req_send, s_sem.at[0])
    wait_bytes(resp_send, s_sem.at[1])
    x_copy.wait_send()
    l_copy.wait_send()
    if owners == n:
        wait_bytes(sm_send.at[pl.ds(0, n - 1)], s_sem.at[2])
        wait_bytes(all_recv.at[pl.ds(0, n - 1)], s_sem.at[4])
    else:
        @pl.when(me < owners)
        def _():
            wait_bytes(sm_send.at[pl.ds(0, owners - 1)], s_sem.at[2])
            wait_bytes(sm_recv, s_sem.at[4])

        @pl.when(me >= owners)
        def _():
            wait_bytes(sm_send.at[pl.ds(0, owners)], s_sem.at[2])
    wait_bytes(big_send.at[pl.ds(0, n - 1)], s_sem.at[3])


def settle(*refs):
    for src, dst in zip(refs[:5], refs[5:]):
        dst[...] = src[...]


def body(tm_n, dp_n, state_feats, achieved, offsets, w_in, b_in, w_out, b_out):
    ep_dev, steps, goal_w = achieved.shape
    feat = state_feats.shape[2]
    rows = ep_dev * steps
    inner, hidden_n = w_in.shape
    n = tm_n * dp_n
    half = hidden_n // dp_n
    rdev = inner // n
    rpad = -(-rdev // 8) * 8
    slots = CAP * (goal_w // LANES)
    owners = 2 * hidden_n // LANES
    assert dp_n == 2 and rows <= 256 and owners <= n and n % GROUP == 0
    vmem = pl.BlockSpec(memory_space=pltpu.VMEM)
    out = pl.pallas_call(
        functools.partial(kernel, (tm_n, dp_n, steps, rdev, rpad)),
        out_shape=(
            jax.ShapeDtypeStruct((steps, ep_dev), F32),
            jax.ShapeDtypeStruct((rdev, hidden_n), F32),
            jax.ShapeDtypeStruct((1, hidden_n), F32),
            jax.ShapeDtypeStruct((1, hidden_n), F32),
            jax.ShapeDtypeStruct((1, 1), F32),
        ),
        in_specs=[pl.BlockSpec(memory_space=pltpu.HBM)] * 6 + [pl.BlockSpec(memory_space=pltpu.SMEM)],
        out_specs=[vmem] * 5,
        scratch_shapes=[
            pltpu.VMEM((ep_dev, steps, feat), BF16),
            pltpu.VMEM((ep_dev, steps, goal_w), BF16),
            pltpu.VMEM((steps, ep_dev), jnp.int32),
            pltpu.VMEM((1, hidden_n), F32),
            pltpu.VMEM((1, hidden_n), F32),
            pltpu.VMEM((inner, hidden_n), BF16),
            pltpu.VMEM((rows, hidden_n), F32),
            pltpu.VMEM((rows, hidden_n), BF16),
            pltpu.VMEM((2, rows, half), BF16),
            pltpu.VMEM((rows, half), BF16),
            pltpu.VMEM((2, n * rpad, rows), BF16),
            pltpu.VMEM((tm_n - 1, slots, LANES), BF16),
            pltpu.VMEM((tm_n - 1, slots, LANES), BF16),
            pltpu.VMEM((tm_n - 1, slots, LANES), BF16),
            pltpu.VMEM((tm_n - 1, slots, LANES), BF16),
            pltpu.VMEM((n, 2 * rpad, half // 2), BF16),
            pltpu.VMEM((n - 1, 2 * rpad, half // 2), BF16),
            pltpu.VMEM((2 * rpad, half // 2), F32),
            pltpu.VMEM((owners, 1, 2 * LANES), F32),
            pltpu.VMEM((n - 1, 1, 2 * LANES), F32),
            pltpu.VMEM((1, 2 * LANES), F32),
            pltpu.VMEM((owners, 1, 2 * LANES), F32),
            pltpu.SemaphoreType.DMA((6,)),
            pltpu.SemaphoreType.DMA((2,)),
            pltpu.SemaphoreType.DMA((2,)),
            pltpu.SemaphoreType.DMA((5,)),
            pltpu.SemaphoreType.DMA((5,)),
        ],
        compiler_params=pltpu.CompilerParams(
            collective_id=0, has_side_effects=True, vmem_limit_bytes=60 * 1024 * 1024),
    )(state_feats, achieved, offsets.T,
      w_in, b_in.reshape(1, hidden_n), w_out.reshape(1, hidden_n), b_out)
    err, gw, gb, gwo, gbo = pl.pallas_call(
        settle,
        out_shape=tuple(jax.ShapeDtypeStruct(o.shape, o.dtype) for o in out),
        in_specs=[vmem] * 5,
        out_specs=[vmem] * 5,
        compiler_params=pltpu.CompilerParams(vmem_limit_bytes=4 * 1024 * 1024),
    )(*out)
    return (err.T, gw, gb.reshape(hidden_n), gwo.reshape(hidden_n), gbo.reshape(1))


def solution(mesh):
    in_specs = (P("dp", "tm", None), P("dp", "tm", None), P("dp", "tm"), P(), P(), P(), P())
    out_specs = (P("dp", "tm"), P(("tm", "dp"), None), P(), P(), P())
    step = functools.partial(body, mesh.shape["tm"], mesh.shape["dp"])
    return jax.shard_map(step, mesh=mesh, in_specs=in_specs, out_specs=out_specs, check_vma=False)
```

```python
import functools
import math

import jax
import jax.numpy as jnp
from jax import lax
from jax.experimental import pallas as pl
from jax.experimental.pallas import tpu as pltpu
from jax.sharding import PartitionSpec as P

CAP = 4
LANES = 128
MESH = pl.DeviceIdType.MESH
BF16 = jnp.bfloat16
F32 = jnp.float32


def iota(shape, axis):
    return lax.broadcasted_iota(jnp.int32, shape, axis)


def dot(a, b):
    return jnp.dot(a, b, preferred_element_type=F32)


def dot_rows(a, b):
    return lax.dot_general(a, b, (((0,), (0,)), ((), ())), preferred_element_type=F32)


def onehot(mask):
    return jnp.where(mask, 1.0, 0.0).astype(BF16)


def wait_bytes(ref, sem):
    pltpu.make_async_copy(ref, ref, sem).wait()


def kernel(dims, sf_hbm, ach_hbm, off_hbm, w_hbm, b_hbm, wo_hbm, bo_ref,
           err_ref, gw_ref, gb_ref, gwo_ref, gbo_ref,
           sf_ref, ach_ref, off_ref, b_ref, wo_ref, w, pre, hid, low, low_send, xt, req_send, req_recv, resp_send, resp_recv,
           near_send, near_recv, far_send, far_recv, mine, sm_send, sm_recv, all_send, all_recv,
           in_sem, pair_send, pair_recv, s_sem, r_sem, near_sem):
    tm_n, dp_n, gsz, steps, rdev, rpad = dims
    groups = tm_n // gsz
    n = tm_n * dp_n
    ep_dev, _, feat = sf_ref.shape
    rows = ep_dev * steps
    goal_w = ach_ref.shape[2]
    hidden_n = wo_ref.shape[1]
    half = hidden_n // dp_n
    inner = feat + goal_w
    nc = goal_w // LANES
    slots = CAP * nc
    peers = tm_n - 1
    tm = lax.axis_index("tm")
    dp = lax.axis_index("dp")
    me = tm * dp_n + dp
    partner = (tm, 1 - dp)

    loads = [pltpu.make_async_copy(src, dst, in_sem.at[j]) for j, (src, dst) in enumerate((
        (off_hbm, off_ref), (ach_hbm, ach_ref), (sf_hbm, sf_ref), (b_hbm, b_ref), (wo_hbm, wo_ref),
        (w_hbm, w)))]
    for load in loads:
        load.start()

    barrier = pltpu.get_barrier_semaphore()

    def greet(k, c):
        dev = lax.rem(me + k, n)
        pl.semaphore_signal(barrier, inc=1, device_id=(dev // dp_n, lax.rem(dev, dp_n)), device_id_type=MESH)
        return c

    lax.fori_loop(1, n, greet, 0)

    def remote(src, dst, ss, rs, dev):
        return pltpu.make_async_remote_copy(
            src_ref=src, dst_ref=dst, send_sem=ss, recv_sem=rs, device_id=dev, device_id_type=MESH)

    loads[0].wait()

    r = iota((1, rows), 1)
    spread = onehot(iota((ep_dev, rows), 0) == iota((ep_dev, rows), 1) // steps)
    off = off_ref[...]
    off = (dot((off // LANES).astype(F32).astype(BF16), spread) * LANES
           + dot(lax.rem(off, LANES).astype(F32).astype(BF16), spread)).astype(jnp.int32)
    off = jnp.sum(jnp.where(iota((steps, rows), 0) == lax.rem(r, steps), off, 0), axis=0, keepdims=True)
    ahead = lax.rem(r, steps) + off
    rel = ahead // steps
    pos = (r // steps) * steps + lax.rem(ahead, steps)
    i = iota((peers * slots, rows), 0)
    hits = (i // slots + 1) == rel
    tri = onehot(iota((rows, rows), 0) <= iota((rows, rows), 1))
    rank = dot(onehot(hits), tri).astype(jnp.int32)
    sel = hits & (rank == lax.rem(i, CAP) + 1)
    want = jnp.sum(jnp.where(sel, pos + 1, 0).astype(F32), axis=1, keepdims=True) - 1.0
    req_send[...] = jnp.broadcast_to(want, (peers * slots, LANES)).astype(BF16).reshape(peers, slots, LANES)

    pl.semaphore_wait(barrier, n - 1)

    def ask(k, c):
        remote(req_send.at[k - 1], req_recv.at[k - 1], s_sem.at[0], r_sem.at[0],
               (lax.rem(tm + k, tm_n), dp)).start()
        return c

    lax.fori_loop(1, tm_n, ask, 0)

    loads[1].wait()
    table = ach_ref[...].reshape(rows, goal_w)
    near = onehot((iota((rows, rows), 0) == pos) & (rel == 0))
    goal_near = dot_rows(near, table)
    loads[2].wait()
    sf = sf_ref[...].reshape(rows, feat)
    if rpad == rdev:
        xt[0, 0:feat, :] = sf.T
    for load in loads[3:]:
        load.wait()
    cw = 256
    chunks = hidden_n // cw

    def first(j, c):
        cols = pl.ds(pl.multiple_of(j * cw, cw), cw)
        pre[:, cols] = dot(sf, w[0:feat, cols]) + b_ref[:, cols]
        return c

    wait_bytes(req_recv, r_sem.at[0])
    asked = req_recv[...].reshape(peers * slots, LANES).astype(F32)
    asked = jnp.concatenate([asked] * (rows // LANES), axis=1).astype(jnp.int32)
    found = asked == iota((peers * slots, rows), 1)
    part = lax.rem(i, slots) // CAP
    picked = jnp.zeros((peers * slots, LANES), F32)
    for c in range(nc):
        picked = picked + dot(onehot(found & (part == c)), table[:, c * LANES:(c + 1) * LANES])
    resp_send[...] = picked.astype(BF16).reshape(peers, slots, LANES)

    def answer(k, c):
        remote(resp_send.at[k - 1], resp_recv.at[k - 1], s_sem.at[1], r_sem.at[1],
               (lax.rem(tm - k + tm_n, tm_n), dp)).start()
        return c

    lax.fori_loop(1, tm_n, answer, 0)
    lax.fori_loop(0, chunks, first, 0)
    wait_bytes(resp_recv, r_sem.at[1])
    fetched = resp_recv[...].reshape(peers * slots, LANES)
    far = [dot_rows(onehot(sel & (part == c)), fetched) for c in range(nc)]
    goal_wide = goal_near + jnp.concatenate(far, axis=1)
    goal = goal_wide.astype(BF16)

    if rpad == rdev:
        xt[0, feat:inner, :] = goal.T
    else:
        x = jnp.concatenate([sf, goal], axis=1)
        o = iota((n * rpad, inner), 0)
        place = (o // rpad) * rdev + lax.rem(o, rpad)
        place = jnp.where(lax.rem(o, rpad) < rdev, place, -1)
        xt[0] = lax.dot_general(onehot(place == iota((n * rpad, inner), 1)), x,
                                (((1,), (1,)), ((), ())), preferred_element_type=F32).astype(BF16)
    x_copy = remote(xt.at[0], xt.at[1], pair_send.at[0], pair_recv.at[0], partner)
    x_copy.start()

    diff = table.astype(F32) - goal_wide
    reward = -jnp.mean(diff * diff, axis=1, keepdims=True)

    def second(j, acc):
        cols = pl.ds(pl.multiple_of(j * cw, cw), cw)
        p = pre[:, cols] + dot(goal, w[feat:inner, cols])
        s = 1.0 / (1.0 + jnp.exp(-p))
        wo = wo_ref[:, cols]
        h = (p * s).astype(BF16)
        hid[:, cols] = h
        pre[:, cols] = wo * (s * (1.0 + p * (1.0 - s)))
        v = h.astype(F32) * wo
        for q in range(cw // LANES):
            acc = acc + v[:, q * LANES:(q + 1) * LANES]
        return acc

    acc = lax.fori_loop(0, chunks, second, jnp.zeros((rows, LANES), F32))
    value = jnp.sum(acc, axis=1, keepdims=True) + bo_ref[0]
    error = value - reward
    er = iota((rows, ep_dev), 0)
    home = er // steps == iota((rows, ep_dev), 1)
    for t in range(steps):
        err_ref[t:t + 1, :] = jnp.sum(
            jnp.where(home & (lax.rem(er, steps) == t), error, 0.0), axis=0, keepdims=True)
    gv = error * (1.0 / math.sqrt(rows * n))
    gbo = jnp.broadcast_to(jnp.sum(gv, axis=0, keepdims=True), (1, LANES))

    per = cw // LANES
    hv = hidden_n // LANES

    def back(which, out):
        def step(j, c):
            col = pl.multiple_of(which * half + j * cw, cw)
            cols = pl.ds(col, cw)
            g = gv * pre[:, cols]
            out[:, pl.ds(pl.multiple_of(j * cw, cw), cw)] = g.astype(BF16)
            gs = jnp.sum(g, axis=0, keepdims=True)
            hs = jnp.sum(gv * hid[:, cols].astype(F32), axis=0, keepdims=True)
            at = which * (half // LANES) + j * per
            for q in range(per):
                lanes = slice(q * LANES, (q + 1) * LANES)
                sm_send[at + q] = jnp.concatenate([gs[:, lanes], gbo], axis=1)
                sm_send[hv + at + q] = jnp.concatenate([hs[:, lanes], gbo], axis=1)
            return c
        return step

    lax.fori_loop(0, half // cw, back(1 - dp, low_send), 0)
    l_copy = remote(low_send, low.at[1], pair_send.at[1], pair_recv.at[1], partner)
    l_copy.start()
    lax.fori_loop(0, half // cw, back(dp, low.at[0]), 0)

    owners = 2 * hv

    def small(k, c):
        dev = lax.rem(me + k, n)

        def go():
            remote(sm_send.at[dev], sm_recv.at[k - 1], s_sem.at[2], r_sem.at[2],
                   (dev // dp_n, lax.rem(dev, dp_n))).start()
        if owners == n:
            go()
        else:
            pl.when(dev < owners)(go)
        return c

    lax.fori_loop(1, n, small, 0)
    x_copy.wait_recv()
    l_copy.wait_recv()

    block = gsz * dp_n * rpad
    outer, place_in = tm // gsz, lax.rem(tm, gsz)

    def form(j, c):
        base = lax.rem(outer + 1 + j, groups)
        at = pl.ds(pl.multiple_of(base * block, block), block)
        p = dot(xt[0, at, :], low[0]) + dot(xt[1, at, :], low[1])
        for t in range(gsz):
            blk = p[t * dp_n * rpad:(t + 1) * dp_n * rpad]
            blk = jnp.concatenate(
                [blk[d * rpad:(d + 1) * rpad, z * (half // 2):(z + 1) * (half // 2)]
                 for d in range(dp_n) for z in range(2)], axis=0)

            @pl.when(place_in == t)
            def _():
                mine[j] = blk

            @pl.when(place_in != t)
            def _():
                k = lax.rem(t - place_in + gsz, gsz)
                near_send[j, k - 1] = blk.astype(BF16)
                remote(near_send.at[j, k - 1], near_recv.at[j, k - 1], s_sem.at[3], near_sem.at[j],
                       (outer * gsz + t, dp)).start()
        return c

    lax.fori_loop(0, groups, form, 0)

    def total():
        wait_bytes(sm_recv, r_sem.at[2])
        all_send[...] = sm_send[me] + jnp.sum(sm_recv[...], axis=0)
        all_recv[me] = all_send[...]

        def tell(k, c):
            dev = lax.rem(me + k, n)
            remote(all_send, all_recv.at[me], s_sem.at[4], r_sem.at[4],
                   (dev // dp_n, lax.rem(dev, dp_n))).start()
            return c

        lax.fori_loop(1, n, tell, 0)

    if owners == n:
        total()
    else:
        pl.when(me < owners)(total)

    def small_out():
        if owners == n:
            wait_bytes(all_recv.at[pl.ds(0, n - 1)], r_sem.at[4])
        else:
            @pl.when(me < owners)
            def _():
                wait_bytes(all_recv.at[pl.ds(0, owners - 1)], r_sem.at[4])

            @pl.when(me >= owners)
            def _():
                wait_bytes(all_recv.at[pl.ds(0, owners)], r_sem.at[4])
        for q in range(hv):
            lanes = slice(q * LANES, (q + 1) * LANES)
            gb_ref[:, lanes] = all_recv[q][:, :LANES]
            gwo_ref[:, lanes] = all_recv[hv + q][:, :LANES]
        gbo_ref[...] = all_recv[0][:, LANES:LANES + 1]

    def gathered(j, rows_at, nrows):
        tot = mine[j, pl.ds(rows_at, nrows), :]
        for k in range(gsz - 1):
            tot = tot + near_recv[j, k, pl.ds(rows_at, nrows), :].astype(F32)
        return tot

    def forward(j, c):
        wait_bytes(near_recv.at[j], near_sem.at[j])
        to = lax.rem(outer + 1 + j, groups) * gsz + place_in
        for d in range(dp_n):
            far_send[j, d] = gathered(j, d * 2 * rpad, 2 * rpad).astype(BF16)
            remote(far_send.at[j, d], far_recv.at[dp_n * j + lax.rem(dp + d, dp_n)], s_sem.at[5], r_sem.at[3],
                   (to, d)).start()
        return c

    last = groups - 1
    lax.fori_loop(0, last, forward, 0)
    wait_bytes(near_recv.at[last], near_sem.at[last])
    far_send[last, 0] = gathered(last, pl.multiple_of((1 - dp) * 2 * rpad, 2 * rpad), 2 * rpad).astype(BF16)
    cross = remote(far_send.at[last, 0], far_recv.at[dp_n * last], pair_send.at[2], pair_recv.at[2], partner)
    cross.start()
    same = gathered(last, pl.multiple_of(dp * 2 * rpad, 2 * rpad), 2 * rpad)
    small_out()
    wait_bytes(far_recv.at[pl.ds(0, dp_n * last)], r_sem.at[3])
    other = jnp.zeros((2 * rpad, half // 2), F32)
    for j in range(last):
        same = same + far_recv[dp_n * j].astype(F32)
        other = other + far_recv[dp_n * j + 1].astype(F32)
    cross.wait_recv()
    other = other + far_recv[dp_n * last].astype(F32)
    for which, val in ((dp, same), (1 - dp, other)):
        for z in range(2):
            col = pl.multiple_of(which * half + z * (half // 2), LANES)
            gw_ref[:, pl.ds(col, half // 2)] = val[z * rpad:z * rpad + rdev]

    wait_bytes(req_send, s_sem.at[0])
    wait_bytes(resp_send, s_sem.at[1])
    x_copy.wait_send()
    l_copy.wait_send()
    if owners == n:
        wait_bytes(sm_send.at[pl.ds(0, n - 1)], s_sem.at[2])
        wait_bytes(all_recv.at[pl.ds(0, n - 1)], s_sem.at[4])
    else:
        @pl.when(me < owners)
        def _():
            wait_bytes(sm_send.at[pl.ds(0, owners - 1)], s_sem.at[2])
            wait_bytes(sm_recv, s_sem.at[4])

        @pl.when(me >= owners)
        def _():
            wait_bytes(sm_send.at[pl.ds(0, owners)], s_sem.at[2])
    wait_bytes(near_send, s_sem.at[3])
    wait_bytes(far_send.at[pl.ds(0, last)], s_sem.at[5])
    cross.wait_send()


def settle(*refs):
    for src, dst in zip(refs[:5], refs[5:]):
        dst[...] = src[...]


def body(tm_n, dp_n, state_feats, achieved, offsets, w_in, b_in, w_out, b_out):
    ep_dev, steps, goal_w = achieved.shape
    feat = state_feats.shape[2]
    rows = ep_dev * steps
    inner, hidden_n = w_in.shape
    n = tm_n * dp_n
    half = hidden_n // dp_n
    rdev = inner // n
    rpad = -(-rdev // 8) * 8
    slots = CAP * (goal_w // LANES)
    owners = 2 * hidden_n // LANES
    gsz = 2 ** (int(math.log2(tm_n)) // 2)
    groups = tm_n // gsz
    piece = 2 * dp_n * rpad
    assert dp_n == 2 and rows <= 256 and owners <= n and tm_n % gsz == 0
    vmem = pl.BlockSpec(memory_space=pltpu.VMEM)
    out = pl.pallas_call(
        functools.partial(kernel, (tm_n, dp_n, gsz, steps, rdev, rpad)),
        out_shape=(
            jax.ShapeDtypeStruct((steps, ep_dev), F32),
            jax.ShapeDtypeStruct((rdev, hidden_n), F32),
            jax.ShapeDtypeStruct((1, hidden_n), F32),
            jax.ShapeDtypeStruct((1, hidden_n), F32),
            jax.ShapeDtypeStruct((1, 1), F32),
        ),
        in_specs=[pl.BlockSpec(memory_space=pltpu.HBM)] * 6 + [pl.BlockSpec(memory_space=pltpu.SMEM)],
        out_specs=[vmem] * 5,
        scratch_shapes=[
            pltpu.VMEM((ep_dev, steps, feat), BF16),
            pltpu.VMEM((ep_dev, steps, goal_w), BF16),
            pltpu.VMEM((steps, ep_dev), jnp.int32),
            pltpu.VMEM((1, hidden_n), F32),
            pltpu.VMEM((1, hidden_n), F32),
            pltpu.VMEM((inner, hidden_n), BF16),
            pltpu.VMEM((rows, hidden_n), F32),
            pltpu.VMEM((rows, hidden_n), BF16),
            pltpu.VMEM((2, rows, half), BF16),
            pltpu.VMEM((rows, half), BF16),
            pltpu.VMEM((2, n * rpad, rows), BF16),
            pltpu.VMEM((tm_n - 1, slots, LANES), BF16),
            pltpu.VMEM((tm_n - 1, slots, LANES), BF16),
            pltpu.VMEM((tm_n - 1, slots, LANES), BF16),
            pltpu.VMEM((tm_n - 1, slots, LANES), BF16),
            pltpu.VMEM((groups, gsz - 1, piece, half // 2), BF16),
            pltpu.VMEM((groups, gsz - 1, piece, half // 2), BF16),
            pltpu.VMEM((groups, dp_n, 2 * rpad, half // 2), BF16),
            pltpu.VMEM((dp_n * (groups - 1) + 1, 2 * rpad, half // 2), BF16),
            pltpu.VMEM((groups, piece, half // 2), F32),
            pltpu.VMEM((owners, 1, 2 * LANES), F32),
            pltpu.VMEM((n - 1, 1, 2 * LANES), F32),
            pltpu.VMEM((1, 2 * LANES), F32),
            pltpu.VMEM((owners, 1, 2 * LANES), F32),
            pltpu.SemaphoreType.DMA((6,)),
            pltpu.SemaphoreType.DMA((3,)),
            pltpu.SemaphoreType.DMA((3,)),
            pltpu.SemaphoreType.DMA((6,)),
            pltpu.SemaphoreType.DMA((5,)),
            pltpu.SemaphoreType.DMA((groups,)),
        ],
        compiler_params=pltpu.CompilerParams(
            collective_id=0, has_side_effects=True, vmem_limit_bytes=60 * 1024 * 1024),
    )(state_feats, achieved, offsets.T,
      w_in, b_in.reshape(1, hidden_n), w_out.reshape(1, hidden_n), b_out)
    err, gw, gb, gwo, gbo = pl.pallas_call(
        settle,
        out_shape=tuple(jax.ShapeDtypeStruct(o.shape, o.dtype) for o in out),
        in_specs=[vmem] * 5,
        out_specs=[vmem] * 5,
        compiler_params=pltpu.CompilerParams(vmem_limit_bytes=60 * 1024 * 1024),
    )(*out)
    return (err.T, gw, gb.reshape(hidden_n), gwo.reshape(hidden_n), gbo.reshape(1))


def solution(mesh):
    in_specs = (P("dp", "tm", None), P("dp", "tm", None), P("dp", "tm"), P(), P(), P(), P())
    out_specs = (P("dp", "tm"), P(("tm", "dp"), None), P(), P(), P())
    step = functools.partial(body, mesh.shape["tm"], mesh.shape["dp"])
    return jax.shard_map(step, mesh=mesh, in_specs=in_specs, out_specs=out_specs, check_vma=False)
```

```python
import functools
import math

import jax
import jax.numpy as jnp
from jax import lax
from jax.experimental import pallas as pl
from jax.experimental.pallas import tpu as pltpu
from jax.sharding import PartitionSpec as P

CAP = 4
LANES = 128
MESH = pl.DeviceIdType.MESH
BF16 = jnp.bfloat16
F32 = jnp.float32


def iota(shape, axis):
    return lax.broadcasted_iota(jnp.int32, shape, axis)


def dot(a, b):
    return jnp.dot(a, b, preferred_element_type=F32)


def dot_rows(a, b):
    return lax.dot_general(a, b, (((0,), (0,)), ((), ())), preferred_element_type=F32)


def onehot(mask):
    return jnp.where(mask, 1.0, 0.0).astype(BF16)


def wait_bytes(ref, sem):
    pltpu.make_async_copy(ref, ref, sem).wait()


def kernel(dims, sf_hbm, ach_hbm, off_hbm, w_hbm, b_hbm, wo_hbm, bo_ref,
           err_ref, gw_ref, gb_ref, gwo_ref, gbo_ref,
           sf_ref, ach_ref, off_ref, b_ref, wo_ref, w, pre, hid, low, low_send, xt, req_send, req_recv, resp_send, resp_recv,
           near_send, near_recv, mid_send, mid_recv, far_send, far_recv, mine, sm_send, sm_recv, all_send, all_recv,
           in_sem, pair_send, pair_recv, s_sem, r_sem, near_sem, mid_sem):
    tm_n, dp_n, gsz, steps, rdev, rpad = dims
    groups = tm_n // gsz
    n = tm_n * dp_n
    ep_dev, _, feat = sf_ref.shape
    rows = ep_dev * steps
    goal_w = ach_ref.shape[2]
    hidden_n = wo_ref.shape[1]
    half = hidden_n // dp_n
    inner = feat + goal_w
    nc = goal_w // LANES
    slots = CAP * nc
    peers = tm_n - 1
    tm = lax.axis_index("tm")
    dp = lax.axis_index("dp")
    me = tm * dp_n + dp
    partner = (tm, 1 - dp)

    loads = [pltpu.make_async_copy(src, dst, in_sem.at[j]) for j, (src, dst) in enumerate((
        (off_hbm, off_ref), (ach_hbm, ach_ref), (sf_hbm, sf_ref), (b_hbm, b_ref), (wo_hbm, wo_ref),
        (w_hbm, w)))]
    for load in loads:
        load.start()

    barrier = pltpu.get_barrier_semaphore()

    def greet(k, c):
        dev = lax.rem(me + k, n)
        pl.semaphore_signal(barrier, inc=1, device_id=(dev // dp_n, lax.rem(dev, dp_n)), device_id_type=MESH)
        return c

    lax.fori_loop(1, n, greet, 0)

    def remote(src, dst, ss, rs, dev):
        return pltpu.make_async_remote_copy(
            src_ref=src, dst_ref=dst, send_sem=ss, recv_sem=rs, device_id=dev, device_id_type=MESH)

    loads[0].wait()

    r = iota((1, rows), 1)
    spread = onehot(iota((ep_dev, rows), 0) == iota((ep_dev, rows), 1) // steps)
    off = off_ref[...]
    off = (dot((off // LANES).astype(F32).astype(BF16), spread) * LANES
           + dot(lax.rem(off, LANES).astype(F32).astype(BF16), spread)).astype(jnp.int32)
    off = jnp.sum(jnp.where(iota((steps, rows), 0) == lax.rem(r, steps), off, 0), axis=0, keepdims=True)
    ahead = lax.rem(r, steps) + off
    rel = ahead // steps
    pos = (r // steps) * steps + lax.rem(ahead, steps)
    i = iota((peers * slots, rows), 0)
    hits = (i // slots + 1) == rel
    tri = onehot(iota((rows, rows), 0) <= iota((rows, rows), 1))
    rank = dot(onehot(hits), tri).astype(jnp.int32)
    sel = hits & (rank == lax.rem(i, CAP) + 1)
    want = jnp.sum(jnp.where(sel, pos + 1, 0).astype(F32), axis=1, keepdims=True) - 1.0
    req_send[...] = jnp.broadcast_to(want, (peers * slots, LANES)).astype(BF16).reshape(peers, slots, LANES)

    pl.semaphore_wait(barrier, n - 1)

    def ask(k, c):
        remote(req_send.at[k - 1], req_recv.at[k - 1], s_sem.at[0], r_sem.at[0],
               (lax.rem(tm + k, tm_n), dp)).start()
        return c

    lax.fori_loop(1, tm_n, ask, 0)

    loads[1].wait()
    table = ach_ref[...].reshape(rows, goal_w)
    near = onehot((iota((rows, rows), 0) == pos) & (rel == 0))
    goal_near = dot_rows(near, table)
    loads[2].wait()
    sf = sf_ref[...].reshape(rows, feat)
    if rpad == rdev:
        xt[0, 0:feat, :] = sf.T
    for load in loads[3:]:
        load.wait()
    cw = 256
    chunks = hidden_n // cw

    def first(j, c):
        cols = pl.ds(pl.multiple_of(j * cw, cw), cw)
        pre[:, cols] = dot(sf, w[0:feat, cols]) + b_ref[:, cols]
        return c

    wait_bytes(req_recv, r_sem.at[0])
    asked = req_recv[...].reshape(peers * slots, LANES).astype(F32)
    asked = jnp.concatenate([asked] * (rows // LANES), axis=1).astype(jnp.int32)
    found = asked == iota((peers * slots, rows), 1)
    part = lax.rem(i, slots) // CAP
    picked = jnp.zeros((peers * slots, LANES), F32)
    for c in range(nc):
        picked = picked + dot(onehot(found & (part == c)), table[:, c * LANES:(c + 1) * LANES])
    resp_send[...] = picked.astype(BF16).reshape(peers, slots, LANES)

    def answer(k, c):
        remote(resp_send.at[k - 1], resp_recv.at[k - 1], s_sem.at[1], r_sem.at[1],
               (lax.rem(tm - k + tm_n, tm_n), dp)).start()
        return c

    lax.fori_loop(1, tm_n, answer, 0)
    lax.fori_loop(0, chunks, first, 0)
    wait_bytes(resp_recv, r_sem.at[1])
    fetched = resp_recv[...].reshape(peers * slots, LANES)
    far = [dot_rows(onehot(sel & (part == c)), fetched) for c in range(nc)]
    goal_wide = goal_near + jnp.concatenate(far, axis=1)
    goal = goal_wide.astype(BF16)

    if rpad == rdev:
        xt[0, feat:inner, :] = goal.T
    else:
        x = jnp.concatenate([sf, goal], axis=1)
        o = iota((n * rpad, inner), 0)
        place = (o // rpad) * rdev + lax.rem(o, rpad)
        place = jnp.where(lax.rem(o, rpad) < rdev, place, -1)
        xt[0] = lax.dot_general(onehot(place == iota((n * rpad, inner), 1)), x,
                                (((1,), (1,)), ((), ())), preferred_element_type=F32).astype(BF16)
    x_copy = remote(xt.at[0], xt.at[1], pair_send.at[0], pair_recv.at[0], partner)
    x_copy.start()

    diff = table.astype(F32) - goal_wide
    reward = -jnp.mean(diff * diff, axis=1, keepdims=True)

    def second(j, acc):
        cols = pl.ds(pl.multiple_of(j * cw, cw), cw)
        p = pre[:, cols] + dot(goal, w[feat:inner, cols])
        s = 1.0 / (1.0 + jnp.exp(-p))
        wo = wo_ref[:, cols]
        h = (p * s).astype(BF16)
        hid[:, cols] = h
        pre[:, cols] = wo * (s * (1.0 + p * (1.0 - s)))
        v = h.astype(F32) * wo
        for q in range(cw // LANES):
            acc = acc + v[:, q * LANES:(q + 1) * LANES]
        return acc

    acc = lax.fori_loop(0, chunks, second, jnp.zeros((rows, LANES), F32))
    value = jnp.sum(acc, axis=1, keepdims=True) + bo_ref[0]
    error = value - reward
    er = iota((rows, ep_dev), 0)
    home = er // steps == iota((rows, ep_dev), 1)
    for t in range(steps):
        err_ref[t:t + 1, :] = jnp.sum(
            jnp.where(home & (lax.rem(er, steps) == t), error, 0.0), axis=0, keepdims=True)
    gv = error * (1.0 / math.sqrt(rows * n))
    gbo = jnp.broadcast_to(jnp.sum(gv, axis=0, keepdims=True), (1, LANES))

    per = cw // LANES
    hv = hidden_n // LANES

    def back(which, out):
        def step(j, c):
            col = pl.multiple_of(which * half + j * cw, cw)
            cols = pl.ds(col, cw)
            g = gv * pre[:, cols]
            out[:, pl.ds(pl.multiple_of(j * cw, cw), cw)] = g.astype(BF16)
            gs = jnp.sum(g, axis=0, keepdims=True)
            hs = jnp.sum(gv * hid[:, cols].astype(F32), axis=0, keepdims=True)
            at = which * (half // LANES) + j * per
            for q in range(per):
                lanes = slice(q * LANES, (q + 1) * LANES)
                sm_send[at + q] = jnp.concatenate([gs[:, lanes], gbo], axis=1)
                sm_send[hv + at + q] = jnp.concatenate([hs[:, lanes], gbo], axis=1)
            return c
        return step

    lax.fori_loop(0, half // cw, back(1 - dp, low_send), 0)
    l_copy = remote(low_send, low.at[1], pair_send.at[1], pair_recv.at[1], partner)
    l_copy.start()
    lax.fori_loop(0, half // cw, back(dp, low.at[0]), 0)

    owners = 2 * hv

    def small(k, c):
        dev = lax.rem(me + k, n)

        def go():
            remote(sm_send.at[dev], sm_recv.at[k - 1], s_sem.at[2], r_sem.at[2],
                   (dev // dp_n, lax.rem(dev, dp_n))).start()
        if owners == n:
            go()
        else:
            pl.when(dev < owners)(go)
        return c

    lax.fori_loop(1, n, small, 0)
    x_copy.wait_recv()
    l_copy.wait_recv()

    block = gsz * dp_n * rpad
    outer, place_in = tm // gsz, lax.rem(tm, gsz)
    flip_low = place_in + 1 - 2 * lax.rem(place_in, 2)
    flip_high = place_in + 2 - 4 * (place_in // 2)
    first_hop = flip_low * (1 - dp) + flip_high * dp
    second_hop = flip_high * (1 - dp) + flip_low * dp

    def form(j, c):
        base = lax.rem(outer + 1 + j, groups)
        at = pl.ds(pl.multiple_of(base * block, block), block)
        p = dot(xt[0, at, :], low[0]) + dot(xt[1, at, :], low[1])
        for t in range(gsz):
            blk = p[t * dp_n * rpad:(t + 1) * dp_n * rpad]
            blk = jnp.concatenate(
                [blk[d * rpad:(d + 1) * rpad, z * (half // 2):(z + 1) * (half // 2)]
                 for d in range(dp_n) for z in range(2)], axis=0)

            @pl.when(place_in == t)
            def _():
                mine[j, 0] = blk

            @pl.when(second_hop == t)
            def _():
                mine[j, 1] = blk

            @pl.when(first_hop == t)
            def _():
                near_send[j, 0] = blk.astype(BF16)

            @pl.when(gsz - 1 - place_in == t)
            def _():
                near_send[j, 1] = blk.astype(BF16)
        remote(near_send.at[j], near_recv.at[j], s_sem.at[3], near_sem.at[j],
               (outer * gsz + first_hop, dp)).start()
        return c

    lax.fori_loop(0, groups, form, 0)

    def total():
        wait_bytes(sm_recv, r_sem.at[2])
        all_send[...] = sm_send[me] + jnp.sum(sm_recv[...], axis=0)
        all_recv[me] = all_send[...]

        def tell(k, c):
            dev = lax.rem(me + k, n)
            remote(all_send, all_recv.at[me], s_sem.at[4], r_sem.at[4],
                   (dev // dp_n, lax.rem(dev, dp_n))).start()
            return c

        lax.fori_loop(1, n, tell, 0)

    if owners == n:
        total()
    else:
        pl.when(me < owners)(total)

    def small_out():
        if owners == n:
            wait_bytes(all_recv.at[pl.ds(0, n - 1)], r_sem.at[4])
        else:
            @pl.when(me < owners)
            def _():
                wait_bytes(all_recv.at[pl.ds(0, owners - 1)], r_sem.at[4])

            @pl.when(me >= owners)
            def _():
                wait_bytes(all_recv.at[pl.ds(0, owners)], r_sem.at[4])
        for q in range(hv):
            lanes = slice(q * LANES, (q + 1) * LANES)
            gb_ref[:, lanes] = all_recv[q][:, :LANES]
            gwo_ref[:, lanes] = all_recv[hv + q][:, :LANES]
        gbo_ref[...] = all_recv[0][:, LANES:LANES + 1]

    def gathered(j, rows_at, nrows):
        at = pl.ds(rows_at, nrows)
        return mine[j, 0, at, :] + near_recv[j, 0, at, :].astype(F32) + mid_recv[j, at, :].astype(F32)

    def relay(j):
        wait_bytes(near_recv.at[j], near_sem.at[j])
        mid_send[j] = (mine[j, 1] + near_recv[j, 1].astype(F32)).astype(BF16)
        remote(mid_send.at[j], mid_recv.at[j], s_sem.at[6], mid_sem.at[j],
               (outer * gsz + second_hop, dp)).start()

    def forward(j, c):
        relay(j + 1)
        wait_bytes(mid_recv.at[j], mid_sem.at[j])
        to = lax.rem(outer + 1 + j, groups) * gsz + place_in
        for d in range(dp_n):
            far_send[j, d] = gathered(j, d * 2 * rpad, 2 * rpad).astype(BF16)
            remote(far_send.at[j, d], far_recv.at[dp_n * j + lax.rem(dp + d, dp_n)], s_sem.at[5], r_sem.at[3],
                   (to, d)).start()
        return c

    last = groups - 1
    relay(0)
    lax.fori_loop(0, last, forward, 0)
    wait_bytes(mid_recv.at[last], mid_sem.at[last])
    far_send[last, 0] = gathered(last, pl.multiple_of((1 - dp) * 2 * rpad, 2 * rpad), 2 * rpad).astype(BF16)
    cross = remote(far_send.at[last, 0], far_recv.at[dp_n * last], pair_send.at[2], pair_recv.at[2], partner)
    cross.start()
    same = gathered(last, pl.multiple_of(dp * 2 * rpad, 2 * rpad), 2 * rpad)
    small_out()
    wait_bytes(far_recv.at[pl.ds(0, dp_n * last)], r_sem.at[3])
    other = jnp.zeros((2 * rpad, half // 2), F32)
    for j in range(last):
        same = same + far_recv[dp_n * j].astype(F32)
        other = other + far_recv[dp_n * j + 1].astype(F32)
    cross.wait_recv()
    other = other + far_recv[dp_n * last].astype(F32)
    for which, val in ((dp, same), (1 - dp, other)):
        for z in range(2):
            col = pl.multiple_of(which * half + z * (half // 2), LANES)
            gw_ref[:, pl.ds(col, half // 2)] = val[z * rpad:z * rpad + rdev]

    wait_bytes(req_send, s_sem.at[0])
    wait_bytes(resp_send, s_sem.at[1])
    x_copy.wait_send()
    l_copy.wait_send()
    if owners == n:
        wait_bytes(sm_send.at[pl.ds(0, n - 1)], s_sem.at[2])
        wait_bytes(all_recv.at[pl.ds(0, n - 1)], s_sem.at[4])
    else:
        @pl.when(me < owners)
        def _():
            wait_bytes(sm_send.at[pl.ds(0, owners - 1)], s_sem.at[2])
            wait_bytes(sm_recv, s_sem.at[4])

        @pl.when(me >= owners)
        def _():
            wait_bytes(sm_send.at[pl.ds(0, owners)], s_sem.at[2])
    wait_bytes(near_send, s_sem.at[3])
    wait_bytes(mid_send, s_sem.at[6])
    wait_bytes(far_send.at[pl.ds(0, last)], s_sem.at[5])
    cross.wait_send()


def settle(*refs):
    for src, dst in zip(refs[:5], refs[5:]):
        dst[...] = src[...]


def body(tm_n, dp_n, state_feats, achieved, offsets, w_in, b_in, w_out, b_out):
    ep_dev, steps, goal_w = achieved.shape
    feat = state_feats.shape[2]
    rows = ep_dev * steps
    inner, hidden_n = w_in.shape
    n = tm_n * dp_n
    half = hidden_n // dp_n
    rdev = inner // n
    rpad = -(-rdev // 8) * 8
    slots = CAP * (goal_w // LANES)
    owners = 2 * hidden_n // LANES
    gsz = 4
    groups = tm_n // gsz
    piece = 2 * dp_n * rpad
    assert dp_n == 2 and rows <= 256 and owners <= n and tm_n % gsz == 0
    vmem = pl.BlockSpec(memory_space=pltpu.VMEM)
    out = pl.pallas_call(
        functools.partial(kernel, (tm_n, dp_n, gsz, steps, rdev, rpad)),
        out_shape=(
            jax.ShapeDtypeStruct((steps, ep_dev), F32),
            jax.ShapeDtypeStruct((rdev, hidden_n), F32),
            jax.ShapeDtypeStruct((1, hidden_n), F32),
            jax.ShapeDtypeStruct((1, hidden_n), F32),
            jax.ShapeDtypeStruct((1, 1), F32),
        ),
        in_specs=[pl.BlockSpec(memory_space=pltpu.HBM)] * 6 + [pl.BlockSpec(memory_space=pltpu.SMEM)],
        out_specs=[vmem] * 5,
        scratch_shapes=[
            pltpu.VMEM((ep_dev, steps, feat), BF16),
            pltpu.VMEM((ep_dev, steps, goal_w), BF16),
            pltpu.VMEM((steps, ep_dev), jnp.int32),
            pltpu.VMEM((1, hidden_n), F32),
            pltpu.VMEM((1, hidden_n), F32),
            pltpu.VMEM((inner, hidden_n), BF16),
            pltpu.VMEM((rows, hidden_n), F32),
            pltpu.VMEM((rows, hidden_n), BF16),
            pltpu.VMEM((2, rows, half), BF16),
            pltpu.VMEM((rows, half), BF16),
            pltpu.VMEM((2, n * rpad, rows), BF16),
            pltpu.VMEM((tm_n - 1, slots, LANES), BF16),
            pltpu.VMEM((tm_n - 1, slots, LANES), BF16),
            pltpu.VMEM((tm_n - 1, slots, LANES), BF16),
            pltpu.VMEM((tm_n - 1, slots, LANES), BF16),
            pltpu.VMEM((groups, 2, piece, half // 2), BF16),
            pltpu.VMEM((groups, 2, piece, half // 2), BF16),
            pltpu.VMEM((groups, piece, half // 2), BF16),
            pltpu.VMEM((groups, piece, half // 2), BF16),
            pltpu.VMEM((groups, dp_n, 2 * rpad, half // 2), BF16),
            pltpu.VMEM((dp_n * (groups - 1) + 1, 2 * rpad, half // 2), BF16),
            pltpu.VMEM((groups, 2, piece, half // 2), F32),
            pltpu.VMEM((owners, 1, 2 * LANES), F32),
            pltpu.VMEM((n - 1, 1, 2 * LANES), F32),
            pltpu.VMEM((1, 2 * LANES), F32),
            pltpu.VMEM((owners, 1, 2 * LANES), F32),
            pltpu.SemaphoreType.DMA((6,)),
            pltpu.SemaphoreType.DMA((3,)),
            pltpu.SemaphoreType.DMA((3,)),
            pltpu.SemaphoreType.DMA((7,)),
            pltpu.SemaphoreType.DMA((5,)),
            pltpu.SemaphoreType.DMA((groups,)),
            pltpu.SemaphoreType.DMA((groups,)),
        ],
        compiler_params=pltpu.CompilerParams(
            collective_id=0, has_side_effects=True, vmem_limit_bytes=60 * 1024 * 1024),
    )(state_feats, achieved, offsets.T,
      w_in, b_in.reshape(1, hidden_n), w_out.reshape(1, hidden_n), b_out)
    err, gw, gb, gwo, gbo = pl.pallas_call(
        settle,
        out_shape=tuple(jax.ShapeDtypeStruct(o.shape, o.dtype) for o in out),
        in_specs=[vmem] * 5,
        out_specs=[vmem] * 5,
        compiler_params=pltpu.CompilerParams(vmem_limit_bytes=60 * 1024 * 1024),
    )(*out)
    return (err.T, gw, gb.reshape(hidden_n), gwo.reshape(hidden_n), gbo.reshape(1))


def solution(mesh):
    in_specs = (P("dp", "tm", None), P("dp", "tm", None), P("dp", "tm"), P(), P(), P(), P())
    out_specs = (P("dp", "tm"), P(("tm", "dp"), None), P(), P(), P())
    step = functools.partial(body, mesh.shape["tm"], mesh.shape["dp"])
    return jax.shard_map(step, mesh=mesh, in_specs=in_specs, out_specs=out_specs, check_vma=False)
```

```python
import functools
import math

import jax
import jax.numpy as jnp
from jax import lax
from jax.experimental import pallas as pl
from jax.experimental.pallas import tpu as pltpu
from jax.sharding import PartitionSpec as P

CAP = 4
LANES = 128
MESH = pl.DeviceIdType.MESH
BF16 = jnp.bfloat16
F32 = jnp.float32


def iota(shape, axis):
    return lax.broadcasted_iota(jnp.int32, shape, axis)


def dot(a, b):
    return jnp.dot(a, b, preferred_element_type=F32)


def dot_rows(a, b):
    return lax.dot_general(a, b, (((0,), (0,)), ((), ())), preferred_element_type=F32)


def onehot(mask):
    return jnp.where(mask, 1.0, 0.0).astype(BF16)


def wait_bytes(ref, sem):
    pltpu.make_async_copy(ref, ref, sem).wait()


def kernel(dims, sf_hbm, ach_hbm, off_hbm, w_hbm, b_hbm, wo_hbm, bo_ref,
           err_ref, gw_ref, gb_ref, gwo_ref, gbo_ref,
           sf_ref, ach_ref, off_ref, b_ref, wo_ref, w, pre, hid, low, low_send, xt, req_send, req_recv, resp_send, resp_recv,
           near_send, near_recv, mid_send, mid_recv, far_send, far_recv, mine, sm_send, sm_recv, all_send, all_recv,
           in_sem, pair_send, pair_recv, s_sem, r_sem, near_sem, mid_sem):
    tm_n, dp_n, gsz, steps, rdev, rpad = dims
    groups = tm_n // gsz
    n = tm_n * dp_n
    ep_dev, _, feat = sf_ref.shape
    rows = ep_dev * steps
    goal_w = ach_ref.shape[2]
    hidden_n = wo_ref.shape[1]
    half = hidden_n // dp_n
    inner = feat + goal_w
    nc = goal_w // LANES
    slots = CAP * nc
    peers = tm_n - 1
    tm = lax.axis_index("tm")
    dp = lax.axis_index("dp")
    me = tm * dp_n + dp
    partner = (tm, 1 - dp)

    loads = [pltpu.make_async_copy(src, dst, in_sem.at[j]) for j, (src, dst) in enumerate((
        (off_hbm, off_ref), (ach_hbm, ach_ref), (sf_hbm, sf_ref), (b_hbm, b_ref), (wo_hbm, wo_ref),
        (w_hbm, w)))]
    for load in loads:
        load.start()

    barrier = pltpu.get_barrier_semaphore()

    def greet(k, c):
        dev = lax.rem(me + k, n)
        pl.semaphore_signal(barrier, inc=1, device_id=(dev // dp_n, lax.rem(dev, dp_n)), device_id_type=MESH)
        return c

    lax.fori_loop(1, n, greet, 0)

    def remote(src, dst, ss, rs, dev):
        return pltpu.make_async_remote_copy(
            src_ref=src, dst_ref=dst, send_sem=ss, recv_sem=rs, device_id=dev, device_id_type=MESH)

    loads[0].wait()

    r = iota((1, rows), 1)
    spread = onehot(iota((ep_dev, rows), 0) == iota((ep_dev, rows), 1) // steps)
    off = off_ref[...]
    off = (dot((off // LANES).astype(F32).astype(BF16), spread) * LANES
           + dot(lax.rem(off, LANES).astype(F32).astype(BF16), spread)).astype(jnp.int32)
    off = jnp.sum(jnp.where(iota((steps, rows), 0) == lax.rem(r, steps), off, 0), axis=0, keepdims=True)
    ahead = lax.rem(r, steps) + off
    rel = ahead // steps
    pos = (r // steps) * steps + lax.rem(ahead, steps)
    i = iota((peers * slots, rows), 0)
    hits = (i // slots + 1) == rel
    tri = onehot(iota((rows, rows), 0) <= iota((rows, rows), 1))
    rank = dot(onehot(hits), tri).astype(jnp.int32)
    sel = hits & (rank == lax.rem(i, CAP) + 1)
    want = jnp.sum(jnp.where(sel, pos + 1, 0).astype(F32), axis=1, keepdims=True) - 1.0
    req_send[...] = jnp.broadcast_to(want, (peers * slots, LANES)).astype(BF16).reshape(peers, slots, LANES)

    pl.semaphore_wait(barrier, n - 1)

    def ask(k, c):
        remote(req_send.at[k - 1], req_recv.at[k - 1], s_sem.at[0], r_sem.at[0],
               (lax.rem(tm + k, tm_n), dp)).start()
        return c

    lax.fori_loop(1, tm_n, ask, 0)

    loads[1].wait()
    table = ach_ref[...].reshape(rows, goal_w)
    near = onehot((iota((rows, rows), 0) == pos) & (rel == 0))
    goal_near = dot_rows(near, table)
    loads[2].wait()
    sf = sf_ref[...].reshape(rows, feat)
    if rpad == rdev:
        xt[0, 0:feat, :] = sf.T
    for load in loads[3:]:
        load.wait()
    cw = 256
    chunks = hidden_n // cw

    def first(j, c):
        cols = pl.ds(pl.multiple_of(j * cw, cw), cw)
        pre[:, cols] = dot(sf, w[0:feat, cols]) + b_ref[:, cols]
        return c

    wait_bytes(req_recv, r_sem.at[0])
    asked = req_recv[...].reshape(peers * slots, LANES).astype(F32)
    asked = jnp.concatenate([asked] * (rows // LANES), axis=1).astype(jnp.int32)
    found = asked == iota((peers * slots, rows), 1)
    part = lax.rem(i, slots) // CAP
    picked = jnp.zeros((peers * slots, LANES), F32)
    for c in range(nc):
        picked = picked + dot(onehot(found & (part == c)), table[:, c * LANES:(c + 1) * LANES])
    resp_send[...] = picked.astype(BF16).reshape(peers, slots, LANES)

    def answer(k, c):
        remote(resp_send.at[k - 1], resp_recv.at[k - 1], s_sem.at[1], r_sem.at[1],
               (lax.rem(tm - k + tm_n, tm_n), dp)).start()
        return c

    lax.fori_loop(1, tm_n, answer, 0)
    lax.fori_loop(0, chunks, first, 0)
    wait_bytes(resp_recv, r_sem.at[1])
    fetched = resp_recv[...].reshape(peers * slots, LANES)
    far = [dot_rows(onehot(sel & (part == c)), fetched) for c in range(nc)]
    goal_wide = goal_near + jnp.concatenate(far, axis=1)
    goal = goal_wide.astype(BF16)

    if rpad == rdev:
        xt[0, feat:inner, :] = goal.T
    else:
        x = jnp.concatenate([sf, goal], axis=1)
        o = iota((n * rpad, inner), 0)
        place = (o // rpad) * rdev + lax.rem(o, rpad)
        place = jnp.where(lax.rem(o, rpad) < rdev, place, -1)
        xt[0] = lax.dot_general(onehot(place == iota((n * rpad, inner), 1)), x,
                                (((1,), (1,)), ((), ())), preferred_element_type=F32).astype(BF16)
    x_copy = remote(xt.at[0], xt.at[1], pair_send.at[0], pair_recv.at[0], partner)
    x_copy.start()

    diff = table.astype(F32) - goal_wide
    reward = -jnp.mean(diff * diff, axis=1, keepdims=True)

    def second(j, acc):
        cols = pl.ds(pl.multiple_of(j * cw, cw), cw)
        p = pre[:, cols] + dot(goal, w[feat:inner, cols])
        s = 1.0 / (1.0 + jnp.exp(-p))
        wo = wo_ref[:, cols]
        h = (p * s).astype(BF16)
        hid[:, cols] = h
        pre[:, cols] = wo * (s * (1.0 + p * (1.0 - s)))
        v = h.astype(F32) * wo
        for q in range(cw // LANES):
            acc = acc + v[:, q * LANES:(q + 1) * LANES]
        return acc

    acc = lax.fori_loop(0, chunks, second, jnp.zeros((rows, LANES), F32))
    value = jnp.sum(acc, axis=1, keepdims=True) + bo_ref[0]
    error = value - reward
    er = iota((rows, ep_dev), 0)
    home = er // steps == iota((rows, ep_dev), 1)
    for t in range(steps):
        err_ref[t:t + 1, :] = jnp.sum(
            jnp.where(home & (lax.rem(er, steps) == t), error, 0.0), axis=0, keepdims=True)
    gv = error * (1.0 / math.sqrt(rows * n))
    gbo = jnp.broadcast_to(jnp.sum(gv, axis=0, keepdims=True), (1, LANES))

    per = cw // LANES
    hv = hidden_n // LANES

    def back(which, out):
        def step(j, c):
            col = pl.multiple_of(which * half + j * cw, cw)
            cols = pl.ds(col, cw)
            g = gv * pre[:, cols]
            out[:, pl.ds(pl.multiple_of(j * cw, cw), cw)] = g.astype(BF16)
            gs = jnp.sum(g, axis=0, keepdims=True)
            hs = jnp.sum(gv * hid[:, cols].astype(F32), axis=0, keepdims=True)
            at = which * (half // LANES) + j * per
            for q in range(per):
                lanes = slice(q * LANES, (q + 1) * LANES)
                sm_send[at + q] = jnp.concatenate([gs[:, lanes], gbo], axis=1)
                sm_send[hv + at + q] = jnp.concatenate([hs[:, lanes], gbo], axis=1)
            return c
        return step

    lax.fori_loop(0, half // cw, back(1 - dp, low_send), 0)
    l_copy = remote(low_send, low.at[1], pair_send.at[1], pair_recv.at[1], partner)
    l_copy.start()
    lax.fori_loop(0, half // cw, back(dp, low.at[0]), 0)

    owners = 2 * hv

    def small(k, c):
        dev = lax.rem(me + k, n)

        def go():
            remote(sm_send.at[dev], sm_recv.at[k - 1], s_sem.at[2], r_sem.at[2],
                   (dev // dp_n, lax.rem(dev, dp_n))).start()
        if owners == n:
            go()
        else:
            pl.when(dev < owners)(go)
        return c

    lax.fori_loop(1, n, small, 0)
    x_copy.wait_recv()
    l_copy.wait_recv()

    block = gsz * dp_n * rpad
    outer, place_in = tm // gsz, lax.rem(tm, gsz)
    flip_low = place_in + 1 - 2 * lax.rem(place_in, 2)
    flip_high = place_in + 2 - 4 * (place_in // 2)
    first_hop = flip_low * (1 - dp) + flip_high * dp
    second_hop = flip_high * (1 - dp) + flip_low * dp

    def form(j, c):
        base = lax.rem(outer + 1 + j, groups)
        at = pl.ds(pl.multiple_of(base * block, block), block)
        p = dot(xt[0, at, :], low[0]) + dot(xt[1, at, :], low[1])
        for t in range(gsz):
            blk = p[t * dp_n * rpad:(t + 1) * dp_n * rpad]
            blk = jnp.concatenate(
                [blk[d * rpad:(d + 1) * rpad, z * (half // 2):(z + 1) * (half // 2)]
                 for d in range(dp_n) for z in range(2)], axis=0)

            @pl.when(place_in == t)
            def _():
                mine[j, 0] = blk

            @pl.when(second_hop == t)
            def _():
                mine[j, 1] = blk

            @pl.when(first_hop == t)
            def _():
                near_send[j, 0] = blk.astype(BF16)

            @pl.when(gsz - 1 - place_in == t)
            def _():
                near_send[j, 1] = blk.astype(BF16)
        remote(near_send.at[j], near_recv.at[j], s_sem.at[3], near_sem.at[j],
               (outer * gsz + first_hop, dp)).start()
        return c

    lax.fori_loop(0, groups, form, 0)

    def total():
        wait_bytes(sm_recv, r_sem.at[2])
        all_send[...] = sm_send[me] + jnp.sum(sm_recv[...], axis=0)
        all_recv[me] = all_send[...]

        def tell(k, c):
            dev = lax.rem(me + k, n)
            remote(all_send, all_recv.at[me], s_sem.at[4], r_sem.at[4],
                   (dev // dp_n, lax.rem(dev, dp_n))).start()
            return c

        lax.fori_loop(1, n, tell, 0)

    def small_out():
        if owners == n:
            wait_bytes(all_recv.at[pl.ds(0, n - 1)], r_sem.at[4])
        else:
            @pl.when(me < owners)
            def _():
                wait_bytes(all_recv.at[pl.ds(0, owners - 1)], r_sem.at[4])

            @pl.when(me >= owners)
            def _():
                wait_bytes(all_recv.at[pl.ds(0, owners)], r_sem.at[4])
        for q in range(hv):
            lanes = slice(q * LANES, (q + 1) * LANES)
            gb_ref[:, lanes] = all_recv[q][:, :LANES]
            gwo_ref[:, lanes] = all_recv[hv + q][:, :LANES]
        gbo_ref[...] = all_recv[0][:, LANES:LANES + 1]

    def gathered(j, rows_at, nrows):
        at = pl.ds(rows_at, nrows)
        return mine[j, 0, at, :] + near_recv[j, 0, at, :].astype(F32) + mid_recv[j, at, :].astype(F32)

    def relay(j):
        wait_bytes(near_recv.at[j], near_sem.at[j])
        mid_send[j] = (mine[j, 1] + near_recv[j, 1].astype(F32)).astype(BF16)
        remote(mid_send.at[j], mid_recv.at[j], s_sem.at[6], mid_sem.at[j],
               (outer * gsz + second_hop, dp)).start()

    def forward(j, c):
        relay(j + 1)
        wait_bytes(mid_recv.at[j], mid_sem.at[j])
        to = lax.rem(outer + 1 + j, groups) * gsz + place_in
        for d in range(dp_n):
            far_send[j, d] = gathered(j, d * 2 * rpad, 2 * rpad).astype(BF16)
            remote(far_send.at[j, d], far_recv.at[dp_n * j + lax.rem(dp + d, dp_n)], s_sem.at[5], r_sem.at[3],
                   (to, d)).start()
        return c

    last = groups - 1
    relay(0)
    lax.fori_loop(0, 1, forward, 0)
    if owners == n:
        total()
    else:
        pl.when(me < owners)(total)
    lax.fori_loop(1, last, forward, 0)
    wait_bytes(mid_recv.at[last], mid_sem.at[last])
    far_send[last, 0] = gathered(last, pl.multiple_of((1 - dp) * 2 * rpad, 2 * rpad), 2 * rpad).astype(BF16)
    cross = remote(far_send.at[last, 0], far_recv.at[dp_n * last], pair_send.at[2], pair_recv.at[2], partner)
    cross.start()
    same = gathered(last, pl.multiple_of(dp * 2 * rpad, 2 * rpad), 2 * rpad)
    small_out()
    wait_bytes(far_recv.at[pl.ds(0, dp_n * last)], r_sem.at[3])
    other = jnp.zeros((2 * rpad, half // 2), F32)
    for j in range(last):
        same = same + far_recv[dp_n * j].astype(F32)
        other = other + far_recv[dp_n * j + 1].astype(F32)
    cross.wait_recv()
    other = other + far_recv[dp_n * last].astype(F32)
    for which, val in ((dp, same), (1 - dp, other)):
        for z in range(2):
            col = pl.multiple_of(which * half + z * (half // 2), LANES)
            gw_ref[:, pl.ds(col, half // 2)] = val[z * rpad:z * rpad + rdev]

    wait_bytes(req_send, s_sem.at[0])
    wait_bytes(resp_send, s_sem.at[1])
    x_copy.wait_send()
    l_copy.wait_send()
    if owners == n:
        wait_bytes(sm_send.at[pl.ds(0, n - 1)], s_sem.at[2])
        wait_bytes(all_recv.at[pl.ds(0, n - 1)], s_sem.at[4])
    else:
        @pl.when(me < owners)
        def _():
            wait_bytes(sm_send.at[pl.ds(0, owners - 1)], s_sem.at[2])
            wait_bytes(sm_recv, s_sem.at[4])

        @pl.when(me >= owners)
        def _():
            wait_bytes(sm_send.at[pl.ds(0, owners)], s_sem.at[2])
    wait_bytes(near_send, s_sem.at[3])
    wait_bytes(mid_send, s_sem.at[6])
    wait_bytes(far_send.at[pl.ds(0, last)], s_sem.at[5])
    cross.wait_send()


def settle(*refs):
    for src, dst in zip(refs[:5], refs[5:]):
        dst[...] = src[...]


def body(tm_n, dp_n, state_feats, achieved, offsets, w_in, b_in, w_out, b_out):
    ep_dev, steps, goal_w = achieved.shape
    feat = state_feats.shape[2]
    rows = ep_dev * steps
    inner, hidden_n = w_in.shape
    n = tm_n * dp_n
    half = hidden_n // dp_n
    rdev = inner // n
    rpad = -(-rdev // 8) * 8
    slots = CAP * (goal_w // LANES)
    owners = 2 * hidden_n // LANES
    gsz = 4
    groups = tm_n // gsz
    piece = 2 * dp_n * rpad
    assert dp_n == 2 and rows <= 256 and owners <= n and tm_n % gsz == 0
    vmem = pl.BlockSpec(memory_space=pltpu.VMEM)
    out = pl.pallas_call(
        functools.partial(kernel, (tm_n, dp_n, gsz, steps, rdev, rpad)),
        out_shape=(
            jax.ShapeDtypeStruct((steps, ep_dev), F32),
            jax.ShapeDtypeStruct((rdev, hidden_n), F32),
            jax.ShapeDtypeStruct((1, hidden_n), F32),
            jax.ShapeDtypeStruct((1, hidden_n), F32),
            jax.ShapeDtypeStruct((1, 1), F32),
        ),
        in_specs=[pl.BlockSpec(memory_space=pltpu.HBM)] * 6 + [pl.BlockSpec(memory_space=pltpu.SMEM)],
        out_specs=[vmem] * 5,
        scratch_shapes=[
            pltpu.VMEM((ep_dev, steps, feat), BF16),
            pltpu.VMEM((ep_dev, steps, goal_w), BF16),
            pltpu.VMEM((steps, ep_dev), jnp.int32),
            pltpu.VMEM((1, hidden_n), F32),
            pltpu.VMEM((1, hidden_n), F32),
            pltpu.VMEM((inner, hidden_n), BF16),
            pltpu.VMEM((rows, hidden_n), F32),
            pltpu.VMEM((rows, hidden_n), BF16),
            pltpu.VMEM((2, rows, half), BF16),
            pltpu.VMEM((rows, half), BF16),
            pltpu.VMEM((2, n * rpad, rows), BF16),
            pltpu.VMEM((tm_n - 1, slots, LANES), BF16),
            pltpu.VMEM((tm_n - 1, slots, LANES), BF16),
            pltpu.VMEM((tm_n - 1, slots, LANES), BF16),
            pltpu.VMEM((tm_n - 1, slots, LANES), BF16),
            pltpu.VMEM((groups, 2, piece, half // 2), BF16),
            pltpu.VMEM((groups, 2, piece, half // 2), BF16),
            pltpu.VMEM((groups, piece, half // 2), BF16),
            pltpu.VMEM((groups, piece, half // 2), BF16),
            pltpu.VMEM((groups, dp_n, 2 * rpad, half // 2), BF16),
            pltpu.VMEM((dp_n * (groups - 1) + 1, 2 * rpad, half // 2), BF16),
            pltpu.VMEM((groups, 2, piece, half // 2), F32),
            pltpu.VMEM((owners, 1, 2 * LANES), F32),
            pltpu.VMEM((n - 1, 1, 2 * LANES), F32),
            pltpu.VMEM((1, 2 * LANES), F32),
            pltpu.VMEM((owners, 1, 2 * LANES), F32),
            pltpu.SemaphoreType.DMA((6,)),
            pltpu.SemaphoreType.DMA((3,)),
            pltpu.SemaphoreType.DMA((3,)),
            pltpu.SemaphoreType.DMA((7,)),
            pltpu.SemaphoreType.DMA((5,)),
            pltpu.SemaphoreType.DMA((groups,)),
            pltpu.SemaphoreType.DMA((groups,)),
        ],
        compiler_params=pltpu.CompilerParams(
            collective_id=0, has_side_effects=True, vmem_limit_bytes=60 * 1024 * 1024),
    )(state_feats, achieved, offsets.T,
      w_in, b_in.reshape(1, hidden_n), w_out.reshape(1, hidden_n), b_out)
    err, gw, gb, gwo, gbo = pl.pallas_call(
        settle,
        out_shape=tuple(jax.ShapeDtypeStruct(o.shape, o.dtype) for o in out),
        in_specs=[vmem] * 5,
        out_specs=[vmem] * 5,
        compiler_params=pltpu.CompilerParams(vmem_limit_bytes=60 * 1024 * 1024),
    )(*out)
    return (err.T, gw, gb.reshape(hidden_n), gwo.reshape(hidden_n), gbo.reshape(1))


def solution(mesh):
    in_specs = (P("dp", "tm", None), P("dp", "tm", None), P("dp", "tm"), P(), P(), P(), P())
    out_specs = (P("dp", "tm"), P(("tm", "dp"), None), P(), P(), P())
    step = functools.partial(body, mesh.shape["tm"], mesh.shape["dp"])
    return jax.shard_map(step, mesh=mesh, in_specs=in_specs, out_specs=out_specs, check_vma=False)
```
